32 devices in a mesh: wide: 8 (over z, x), narrow: 4 (over y, core).
Axes of the slice: x: 2, y: 2, z: 4, core: 2. Of those that a mesh axis runs over, the one named last changes fastest.
Arguments:
- tokens: bfloat16 [32768, 1024], P(('wide', 'narrow')), may hold values from -6 to 6
- seg_ids: int32 [32, 1024], P(('wide', 'narrow')), may hold values from 0 to 7, never falling along the last dimension, each value on 1 to 512 neighbouring positions
- ln_gain: bfloat16 [1024], replicated, may hold values from 0.099609375 to 1.8984375
- ln_bias: bfloat16 [1024], replicated, may hold values from -3 to 3
- w_qkv: bfloat16 [1024, 3072], replicated, may hold values from -0.1875 to 0.1875
- b_qkv: bfloat16 [3072], replicated, may hold values from -3 to 3
- w_dense: bfloat16 [1024, 1024], replicated, may hold values from -0.75 to 0.75
- w_up: bfloat16 [1024, 4096], P(None, 'narrow'), may hold values from -0.1875 to 0.1875
- b_up: bfloat16 [4096], P('narrow'), may hold values from -3 to 3
- w_down: bfloat16 [4096, 1024], P('narrow'), may hold values from -0.09375 to 0.09375
- out_bias: bfloat16 [1024], replicated, may hold values from -3 to 3
- cotangent: bfloat16 [32768, 1024], P(('wide', 'narrow')), may hold values from -6 to 6
Outputs:
- mixed: bfloat16 [32768, 1024], P(('wide', 'narrow'))
- d_tokens: bfloat16 [32768, 1024], P(('wide', 'narrow'))
- d_ln_gain: float32 [1024], P('narrow')
- d_ln_bias: float32 [1024], P('narrow')
- d_w_qkv: float32 [1024, 3072], P(None, 'narrow')
- d_b_qkv: float32 [3072], P('narrow')
- d_w_dense: float32 [1024, 1024], P('narrow')
- d_w_up: float32 [1024, 4096], P(None, 'narrow')
- d_b_up: float32 [4096], P('narrow')
- d_w_down: float32 [4096, 1024], P('narrow')
- d_out_bias: float32 [1024], P('narrow')
The draws below stay inside these ranges and needn't reach their ends.
Inputs may be any that keep to these rules, and one draw needn't show every extreme that they name: `seg_ids`: within each sequence of 1024 tokens the document numbers never fall; each document holds 1 to 512 tokens, and one holds exactly 512.
All inputs are finite; a program needn't handle non-finite values.
Results may differ from the reference program's by a relative error of at most 0.011.
Values may be sent and summed in bfloat16 or wider, within the bound.
A program may use at most 320 MiB of HBM per device.

```python
import math
import jax
import jax.numpy as jnp
import numpy as np
from jax import lax

D = 1024
HEADS = 16
HEAD = 64
ROT = 16
FF = 4096
SEQ = 1024
DOCS = 8
SEQS = 32
TOKENS = 32768
N_NARROW = 4


def shard_levels(rng, extent, shards, low, top_value):
    factor_of, own = 1.0, jax.random.fold_in(rng, 6)
    for dim, blocks in shards:
        steps = jnp.exp(jax.random.uniform(jax.random.fold_in(own, dim), (blocks,), jnp.float32, low / len(shards), top_value / len(shards)))
        factor_of = factor_of * jnp.repeat(steps, extent[dim] // blocks).reshape([-1 if axis == dim else 1 for axis in range(len(extent))])
    return factor_of


def split_up(amount, total, reach, lean):
    weights = [(1 << 20) // math.isqrt(rank ** lean) + 1 for rank in range(2, amount + 1)]
    surplus, holding = total - reach - (amount - 1), [1] * (amount - 1)
    while surplus > 0:
        movable = [i for i in range(amount - 1) if holding[i] < reach]
        mass, remaining = sum([weights[i] for i in movable]), surplus
        for i in movable:
            extra = min(reach - holding[i], max(1, remaining * weights[i] // mass), surplus)
            holding[i] = holding[i] + extra
            surplus = surplus - extra
    return np.array([reach] + holding)


def ragged_sizes(rng, number_of, total, most, lean):
    if number_of == 2:
        one = jax.random.randint(rng, (), max(1, total - most), min(most, total - 1) + 1)
        return jnp.stack([one, total - one])
    tallies = jnp.asarray(split_up(number_of, total, most, lean), jnp.int32)
    pairs = (number_of - 1) // 2
    giver, taker = tallies[1:1 + 2 * pairs:2], tallies[2:2 + 2 * pairs:2]
    slack = jnp.minimum(giver - 1, most - taker)
    moved = jax.random.randint(jax.random.fold_in(rng, 1), (pairs,), 0, 1 << 20) % (slack + 1)
    tallies = tallies.at[1:1 + 2 * pairs:2].set(giver - moved).at[2:2 + 2 * pairs:2].set(taker + moved)
    return tallies[jax.random.permutation(jax.random.fold_in(rng, 2), number_of)]


def normal_values(rng, extent, width, reach, cuts=(), kind=jnp.bfloat16):
    level = shard_levels(rng, extent, cuts, -0.22, 0.18) if cuts else 1.0
    entries = jax.random.normal(rng, extent, jnp.float32) * width * level
    return jnp.minimum(jnp.maximum(entries, -reach), reach).astype(kind)


def setup_inputs(seed: int = 0) -> dict:
    streams_of = jax.random.split(jax.random.key(seed), 13)
    tokens = normal_values(streams_of[0], (TOKENS, D), 1.0, 6.0, ((0, 32),))
    seg_ids = jax.vmap(lambda own: jnp.searchsorted(jnp.cumsum(ragged_sizes(own, DOCS, SEQ, SEQ // 2, 1)), jnp.arange(SEQ), side="right"))(jax.random.split(streams_of[1], SEQS)).reshape((SEQS, SEQ)).astype(jnp.int32)
    ln_gain = jnp.clip(1.0 + 0.18 * jax.random.normal(streams_of[2], (D,), jnp.float32), 0.099609375, 1.8984375).astype(jnp.bfloat16)
    ln_bias = normal_values(streams_of[3], (D,), 0.5, 3.0)
    w_qkv = normal_values(streams_of[4], (D, 3 * D), D ** -0.5, 0.1875)
    b_qkv = normal_values(streams_of[5], (3 * D,), 0.5, 3.0)
    w_dense = normal_values(streams_of[6], (D, D), (D // 16) ** -0.5, 0.75)
    w_up = normal_values(streams_of[7], (D, FF), D ** -0.5, 0.1875, ((1, 4),))
    b_up = normal_values(streams_of[8], (FF,), 0.5, 3.0, ((0, 4),))
    w_down = normal_values(streams_of[9], (FF, D), FF ** -0.5, 0.09375, ((0, 4),))
    out_bias = normal_values(streams_of[10], (D,), 0.5, 3.0)
    cotangent = normal_values(streams_of[11], (TOKENS, D), 1.0, 6.0, ((0, 32),))
    return dict(tokens=tokens, seg_ids=seg_ids, ln_gain=ln_gain, ln_bias=ln_bias, w_qkv=w_qkv, b_qkv=b_qkv, w_dense=w_dense, w_up=w_up, b_up=b_up, w_down=w_down, out_bias=out_bias, cotangent=cotangent)


@jax.custom_vjp
def low(v):
    return lax.optimization_barrier(v.astype(jnp.bfloat16)).astype(jnp.float32)

@jax.custom_vjp
def low_back(v):
    return v

def low_keep(v):
    return (low(v), None)

def low_pass(kept, grad):
    return (grad,)

def back_keep(v):
    return (v, None)

def back_low(kept, grad):
    return (low(grad),)
low.defvjp(low_keep, low_pass)
low_back.defvjp(back_keep, back_low)

def positions(segments):
    index_row = jnp.arange(segments.shape[0], dtype=jnp.int32)
    change = jnp.concatenate([jnp.ones((1,), dtype=jnp.bool_), segments[1:] != segments[:-1]])
    first_index = jnp.where(change, index_row, 0).astype(jnp.int32)
    return index_row - lax.cummax(first_index, axis=0)

def rope_tables(position):
    half_rot = ROT // 2
    inv_freq = 1.0 / 10000.0 ** (jnp.arange(half_rot, dtype=jnp.float32) * 2.0 / ROT)
    angles = position.astype(jnp.float32)[:, None] * inv_freq[None, :]
    angles = jnp.concatenate([angles, angles], axis=1)
    return (jnp.cos(angles), jnp.sin(angles))

def rotate(tensor, cos_table, sin_table):
    half_rot = ROT // 2
    rot_part = tensor[..., :ROT]
    turned = jnp.concatenate([-rot_part[..., half_rot:], rot_part[..., :half_rot]], axis=-1)
    rot_part = rot_part * cos_table[..., None, :] + turned * sin_table[..., None, :]
    return jnp.concatenate([rot_part, tensor[..., ROT:]], axis=-1)

def attend(proj_seq, segments):
    highest = lax.Precision.HIGHEST
    split_qkv = proj_seq.reshape(SEQ, 3, HEADS, HEAD)
    cos_table, sin_table = rope_tables(positions(segments))
    queries = low(rotate(split_qkv[:, 0], cos_table, sin_table))
    keys_rot = low(rotate(split_qkv[:, 1], cos_table, sin_table))
    values_low = low(split_qkv[:, 2])
    raw_scores = jnp.einsum('qhd,khd->hqk', queries, keys_rot, precision=highest) * (1.0 / math.sqrt(HEAD))
    scores = low_back(raw_scores)
    index_row = jnp.arange(SEQ, dtype=jnp.int32)
    visible = (segments[:, None] == segments[None, :]) & (index_row[None, :] <= index_row[:, None])
    scores = jnp.where(visible[None], scores, -1e+30)
    probs = low(jax.nn.softmax(scores, axis=-1))
    output = jnp.einsum('hqk,khd->qhd', probs, values_low, precision=highest)
    return low_back(low(output.reshape(SEQ, D)))

def forward(tok_f32, ln_gain, ln_bias, w_qkv, b_qkv, w_dense, w_up, b_up, w_down, out_bias, segments):
    highest = lax.Precision.HIGHEST
    row_mean = lax.optimization_barrier(jnp.mean(tok_f32, axis=-1, keepdims=True))
    centered = tok_f32 - row_mean
    variance = lax.optimization_barrier(jnp.mean(centered * centered, axis=-1, keepdims=True))
    normed = low(centered * lax.rsqrt(variance + 1e-05) * ln_gain + ln_bias)
    proj = low_back(jnp.dot(normed, w_qkv, precision=highest) + b_qkv)
    attended = lax.map(jax.checkpoint(lambda pair: attend(pair[0], pair[1])), (proj.reshape(-1, SEQ, 3 * D), segments))
    attn_out = jnp.dot(attended.reshape(-1, D), w_dense, precision=highest)
    slice_width = FF // N_NARROW
    mlp_out = jnp.zeros_like(tok_f32)
    for slot in range(N_NARROW):
        lower = slot * slice_width
        normed_slice = low_back(normed)
        pre_act = low_back(jnp.dot(normed_slice, w_up[:, lower:lower + slice_width], precision=highest) + b_up[lower:lower + slice_width])
        hidden = low(jax.nn.gelu(pre_act, approximate=False))
        mlp_out = mlp_out + low(jnp.dot(hidden, w_down[lower:lower + slice_width], precision=highest))
    return tok_f32 + attn_out + mlp_out + out_bias

def reference(tokens, seg_ids, ln_gain, ln_bias, w_qkv, b_qkv, w_dense, w_up, b_up, w_down, out_bias, cotangent):
    weights_f32 = tuple((a.astype(jnp.float32) for a in (ln_gain, ln_bias, w_qkv, b_qkv, w_dense, w_up, b_up, w_down, out_bias)))
    group_seqs = math.gcd(SEQS, max(1, 4096 // SEQ))
    tok_groups = tokens.reshape(-1, group_seqs * SEQ, D)
    seg_groups = seg_ids.reshape(-1, group_seqs, SEQ)
    cot_groups = cotangent.reshape(-1, group_seqs * SEQ, D)

    def group_step(totals, group_item):
        tok_group, seg_group, cot_group = group_item

        def forward_fn(tok_f32, *weights):
            return forward(tok_f32, *weights, seg_group)
        mixed, pullback = jax.vjp(forward_fn, tok_group.astype(jnp.float32), *weights_f32)
        grads = pullback(cot_group.astype(jnp.float32))
        totals = tuple((a + b for a, b in zip(totals, grads[1:])))
        return (totals, (mixed.astype(jnp.bfloat16), grads[0].astype(jnp.bfloat16)))
    start_totals = tuple((jnp.zeros_like(a) for a in weights_f32))
    totals, (mixed, d_tokens) = lax.scan(group_step, start_totals, (tok_groups, seg_groups, cot_groups))
    d_ln_gain, d_ln_bias, d_w_qkv, d_b_qkv, d_w_dense, d_w_up, d_b_up, d_w_down, d_out_bias = totals
    return (mixed.reshape(-1, D), d_tokens.reshape(-1, D), d_ln_gain, d_ln_bias, d_w_qkv, d_b_qkv, d_w_dense, d_w_up, d_b_up, d_w_down, d_out_bias)
```

```python
import math

import jax
import jax.numpy as jnp
from jax import lax
from jax.experimental import pallas as pl
from jax.experimental.pallas import tpu as pltpu
from jax.sharding import PartitionSpec as P

D = 1024
HEADS = 16
HEAD = 64
ROT = 16


TILE = 256
PAIR = 2 * HEAD
MAX_DOC = 512


def doc_starts(segments):
    return jnp.sum((segments[:, :, None] > segments[:, None, :]).astype(jnp.int32), axis=2)


def rope_coefs(position):
    half_rot = ROT // 2
    lane = jnp.arange(PAIR, dtype=jnp.int32) % HEAD
    inv_freq = 1.0 / 10000.0 ** ((lane % half_rot).astype(jnp.float32) * 2.0 / ROT)
    angles = position.astype(jnp.float32)[:, None] * inv_freq[None, :]
    cos, sin = jnp.cos(angles), jnp.sin(angles)
    rotated = (lane < ROT)[None, :]
    first = (lane < half_rot)[None, :]
    return (
        jnp.where(rotated, cos, 1.0),
        jnp.where(first, -sin, 0.0),
        jnp.where(rotated & ~first, sin, 0.0),
    )


def turn(t, same, down, up):
    half_rot = ROT // 2
    return (
        t * same
        + pltpu.roll(t, PAIR - half_rot, axis=1) * down
        + pltpu.roll(t, half_rot, axis=1) * up
    )


def dot_nt(left, right):
    return lax.dot_general(
        left, right, (((1,), (1,)), ((), ())), preferred_element_type=jnp.float32
    )


def dot_nn(left, right):
    return lax.dot_general(
        left, right, (((1,), (0,)), ((), ())), preferred_element_type=jnp.float32
    )


def qkv_kernel(
    x_ref, gain_ref, bias_ref, w_ref, b_ref, same_ref, down_ref, up_ref, out_ref, normed_ref
):
    step = pl.program_id(0)
    rows, cols = out_ref.shape
    blocks = (HEADS * HEAD) // cols

    @pl.when(step == 0)
    def _():
        for r in range(0, rows, TILE):
            x = x_ref[r : r + TILE, :].astype(jnp.float32)
            mean = jnp.mean(x, axis=-1, keepdims=True)
            centered = x - mean
            variance = jnp.mean(centered * centered, axis=-1, keepdims=True)
            unit = centered * lax.rsqrt(variance + 1e-05)
            normed_ref[r : r + TILE, :] = (unit * gain_ref[...] + bias_ref[...]).astype(
                jnp.bfloat16
            )

    scale = jnp.where(step < blocks, 1.0 / math.sqrt(HEAD), 1.0)
    for r in range(0, rows, TILE):
        acc = dot_nn(normed_ref[r : r + TILE, :], w_ref[...]) + b_ref[...]

        @pl.when(step < 2 * blocks)
        def _():
            same = same_ref[r : r + TILE, :]
            down = down_ref[r : r + TILE, :]
            up = up_ref[r : r + TILE, :]
            for c in range(0, cols, PAIR):
                out_ref[r : r + TILE, c : c + PAIR] = (
                    turn(acc[:, c : c + PAIR], same, down, up) * scale
                ).astype(jnp.bfloat16)

        @pl.when(step >= 2 * blocks)
        def _():
            out_ref[r : r + TILE, :] = acc.astype(jnp.bfloat16)


def project(tokens, gain, bias, w_qkv, b_qkv, coefs):
    rows, width = tokens.shape
    cols = 512
    whole = lambda shape: pl.BlockSpec(shape, lambda j: (0, 0))
    return pl.pallas_call(
        qkv_kernel,
        grid=(w_qkv.shape[1] // cols,),
        in_specs=[
            whole((rows, width)),
            whole((1, width)),
            whole((1, width)),
            pl.BlockSpec((width, cols), lambda j: (0, j)),
            pl.BlockSpec((1, cols), lambda j: (0, j)),
            whole((rows, PAIR)),
            whole((rows, PAIR)),
            whole((rows, PAIR)),
        ],
        out_specs=[pl.BlockSpec((rows, cols), lambda j: (0, j)), whole((rows, width))],
        out_shape=[
            jax.ShapeDtypeStruct((rows, w_qkv.shape[1]), jnp.bfloat16),
            jax.ShapeDtypeStruct((rows, width), jnp.bfloat16),
        ],
        compiler_params=pltpu.CompilerParams(vmem_limit_bytes=40 << 20),
        cost_estimate=pl.CostEstimate(
            flops=2 * rows * width * w_qkv.shape[1],
            bytes_accessed=2 * (rows * width * 2 + width * w_qkv.shape[1] * 2),
            transcendentals=0,
        ),
    )(tokens, gain, bias, w_qkv, b_qkv, *coefs)


def attention_kernel(
    first_ref,
    start_ref,
    q_ref,
    k_ref,
    v_ref,
    g_ref,
    same_ref,
    down_ref,
    up_ref,
    att_ref,
    grad_ref,
    dk_acc,
    dv_acc,
    kt_ref,
    vt_ref,
):
    rows = q_ref.shape[0]
    lane = lax.broadcasted_iota(jnp.int32, (1, PAIR), 1)
    dk_acc[...] = jnp.zeros_like(dk_acc)
    dv_acc[...] = jnp.zeros_like(dv_acc)
    kt_ref[...] = k_ref[...].astype(jnp.float32).T.astype(jnp.bfloat16)
    vt_ref[...] = v_ref[...].astype(jnp.float32).T.astype(jnp.bfloat16)

    def one_block(block, first, count):
        at = pl.multiple_of(block * TILE, TILE)
        here = pl.ds(at, TILE)
        q_pair, g_pair = q_ref[here, :], g_ref[here, :]
        start = start_ref[:, here]
        query_index = at + lax.broadcasted_iota(jnp.int32, (1, TILE), 1)
        keys = [
            pl.ds(pl.multiple_of((first + j) * TILE, TILE), TILE) for j in range(count)
        ]
        key_index = [
            (first + j) * TILE + lax.broadcasted_iota(jnp.int32, (TILE, TILE), 0)
            for j in range(count)
        ]
        visible = [(idx >= start) & (idx <= query_index) for idx in key_index]
        out_t, dq_t = [], []
        for head in range(2):
            mine = (lane >= head * HEAD) & (lane < (head + 1) * HEAD)
            q = jnp.where(mine, q_pair, jnp.zeros_like(q_pair))
            g = jnp.where(mine, g_pair, jnp.zeros_like(g_pair))
            wide = slice(head * HEAD, (head + 1) * HEAD)
            scores = [
                jnp.where(visible[j], dot_nt(k_ref[keys[j], :], q), -1e30) for j in range(count)
            ]
            grad_prob = [dot_nt(v_ref[keys[j], :], g) for j in range(count)]
            top = jnp.max(scores[0], axis=0, keepdims=True)
            for j in range(1, count):
                top = jnp.maximum(top, jnp.max(scores[j], axis=0, keepdims=True))
            exps = [jnp.exp(s - top) for s in scores]
            total = sum(jnp.sum(e, axis=0, keepdims=True) for e in exps)
            inverse = 1.0 / total
            probs = [e * inverse for e in exps]
            row_dot = sum(
                jnp.sum(p * d, axis=0, keepdims=True) for p, d in zip(probs, grad_prob)
            )
            out_head = jnp.zeros((HEAD, TILE), jnp.float32)
            dq_head = jnp.zeros((HEAD, TILE), jnp.float32)
            for j in range(count):
                low = probs[j].astype(jnp.bfloat16)
                grad_score = (probs[j] * (grad_prob[j] - row_dot)).astype(jnp.bfloat16)
                out_head += dot_nn(vt_ref[wide, keys[j]], low)
                dq_head += dot_nn(kt_ref[wide, keys[j]], grad_score)
                dv_acc[keys[j], :] += dot_nn(low, g)
                dk_acc[keys[j], :] += dot_nn(grad_score, q)
            out_t.append(out_head)
            dq_t.append(dq_head)
        att_ref[here, :] = jnp.concatenate(out_t, axis=0).T.astype(jnp.bfloat16)
        dq = jnp.concatenate(dq_t, axis=0).T * (1.0 / math.sqrt(HEAD))
        grad_ref[0, here, :] = turn(
            dq, same_ref[here, :], -down_ref[here, :], -up_ref[here, :]
        ).astype(jnp.bfloat16)

    span = MAX_DOC // TILE + 1

    def step(block, carry):
        first = first_ref[block]
        count = block + 1 - first
        for n in range(1, span + 1):

            @pl.when(count == n)
            def _(n=n):
                one_block(block, first, n)

        return carry

    lax.fori_loop(0, rows // TILE, step, 0)
    grad_ref[1] = turn(dk_acc[...], same_ref[...], -down_ref[...], -up_ref[...]).astype(
        jnp.bfloat16
    )
    grad_ref[2] = dv_acc[...].astype(jnp.bfloat16)


def attend(qkv, grad_att, starts, coefs):
    rows = qkv.shape[0]
    width = HEADS * HEAD
    pairs = width // PAIR
    first = starts[::TILE] // TILE
    whole = pl.BlockSpec((rows, PAIR), lambda i, f: (0, 0))
    return pl.pallas_call(
        attention_kernel,
        grid_spec=pltpu.PrefetchScalarGridSpec(
            num_scalar_prefetch=1,
            grid=(pairs,),
            in_specs=[
                pl.BlockSpec((1, rows), lambda i, f: (0, 0)),
                pl.BlockSpec((rows, PAIR), lambda i, f: (0, i)),
                pl.BlockSpec((rows, PAIR), lambda i, f: (0, pairs + i)),
                pl.BlockSpec((rows, PAIR), lambda i, f: (0, 2 * pairs + i)),
                pl.BlockSpec((rows, PAIR), lambda i, f: (0, i)),
                whole,
                whole,
                whole,
            ],
            out_specs=[
                pl.BlockSpec((rows, PAIR), lambda i, f: (0, i)),
                pl.BlockSpec((3, rows, PAIR), lambda i, f: (0, 0, i)),
            ],
            scratch_shapes=[
                pltpu.VMEM((rows, PAIR), jnp.float32),
                pltpu.VMEM((rows, PAIR), jnp.float32),
                pltpu.VMEM((PAIR, rows), jnp.bfloat16),
                pltpu.VMEM((PAIR, rows), jnp.bfloat16),
            ],
        ),
        out_shape=[
            jax.ShapeDtypeStruct((rows, width), jnp.bfloat16),
            jax.ShapeDtypeStruct((3, rows, width), jnp.bfloat16),
        ],
        compiler_params=pltpu.CompilerParams(vmem_limit_bytes=40 << 20),
        cost_estimate=pl.CostEstimate(
            flops=16 * rows * rows * width, bytes_accessed=16 * rows * width, transcendentals=0
        ),
    )(first, starts[None, :], qkv, qkv, qkv, grad_att, *coefs)


def contract_rows(left, right):
    return lax.dot_general(
        left, right, (((0,), (0,)), ((), ())), preferred_element_type=jnp.float32
    )


def contract_cols(left, right):
    return lax.dot_general(
        left, right, (((1,), (1,)), ((), ())), preferred_element_type=jnp.float32
    )


def exact_gelu(values_in):
    return jax.nn.gelu(values_in, approximate=False)


def body(
    tokens,
    seg_ids,
    ln_gain,
    ln_bias,
    w_qkv,
    b_qkv,
    w_dense,
    w_up,
    b_up,
    w_down,
    out_bias,
    cotangent,
):
    tok_rows, model_width = tokens.shape
    seq_count, seq_len = seg_ids.shape
    tok_f32 = tokens.astype(jnp.float32)
    row_mean = jnp.mean(tok_f32, axis=-1, keepdims=True)
    centered = tok_f32 - row_mean
    variance = jnp.mean(centered * centered, axis=-1, keepdims=True)
    inv_std = lax.rsqrt(variance + 1e-05)
    unit_rows = centered * inv_std
    gain_f32 = ln_gain.astype(jnp.float32)
    starts = doc_starts(seg_ids)
    position = jnp.arange(seq_len, dtype=jnp.int32)[None, :] - starts
    grad_att = contract_cols(cotangent, w_dense).astype(jnp.bfloat16)
    pieces = []
    for s in range(seq_count):
        part = slice(s * seq_len, (s + 1) * seq_len)
        coefs = rope_coefs(position[s])
        qkv, normed_part = project(
            tokens[part],
            gain_f32[None, :],
            ln_bias.astype(jnp.float32)[None, :],
            w_qkv,
            b_qkv.astype(jnp.float32)[None, :],
            coefs,
        )
        att_part, grad_part = attend(qkv, grad_att[part], starts[s], coefs)
        pieces.append((normed_part, att_part, grad_part))
    normed_low, attended_low = (
        jnp.concatenate([p[i] for p in pieces], axis=0) for i in range(2)
    )
    grad_proj = jnp.concatenate([p[2] for p in pieces], axis=1)
    grad_proj = jnp.concatenate([grad_proj[i] for i in range(3)], axis=1)
    attn_out = jnp.dot(attended_low, w_dense, preferred_element_type=jnp.float32)
    normed_all = lax.all_gather(normed_low, "narrow", axis=0, tiled=True)
    pre_act = jnp.dot(normed_all, w_up, preferred_element_type=jnp.float32) + b_up.astype(
        jnp.float32
    )
    hidden = exact_gelu(pre_act).astype(jnp.bfloat16)
    row_piece = hidden
    partial_low = jnp.dot(row_piece, w_down, preferred_element_type=jnp.float32).astype(
        jnp.bfloat16
    )
    mlp_out = lax.psum_scatter(
        lax.optimization_barrier(partial_low).astype(jnp.float32).astype(jnp.bfloat16),
        "narrow",
        scatter_dimension=0,
        tiled=True,
    ).astype(jnp.float32)
    mixed = (tok_f32 + attn_out + mlp_out + out_bias.astype(jnp.float32)).astype(jnp.bfloat16)
    grad_f32 = cotangent.astype(jnp.float32)
    d_out_bias = jnp.sum(grad_f32, axis=0)
    d_w_dense = contract_rows(attended_low, cotangent)
    d_w_qkv = contract_rows(normed_low, grad_proj)
    d_b_qkv = jnp.sum(grad_proj.astype(jnp.float32), axis=0)
    grad_normed = contract_cols(grad_proj, w_qkv)
    grad_all = lax.all_gather(cotangent, "narrow", axis=0, tiled=True)
    grad_hidden = contract_cols(grad_all, w_down)
    unused, gelu_pull = jax.vjp(exact_gelu, pre_act)
    grad_pre = gelu_pull(grad_hidden)[0].astype(jnp.bfloat16)
    d_w_down = contract_rows(hidden, grad_all)
    d_w_up = contract_rows(normed_all, grad_pre)
    d_b_up = jnp.sum(grad_pre.astype(jnp.float32), axis=0)
    row_piece = grad_pre
    partial_low = contract_cols(row_piece, w_up).astype(jnp.bfloat16)
    grad_normed = grad_normed + lax.psum_scatter(
        lax.optimization_barrier(partial_low).astype(jnp.float32).astype(jnp.bfloat16),
        "narrow",
        scatter_dimension=0,
        tiled=True,
    ).astype(jnp.float32)
    grad_unit = grad_normed * gain_f32
    d_ln_gain = jnp.sum(grad_normed * unit_rows, axis=0)
    d_ln_bias = jnp.sum(grad_normed, axis=0)
    mean_grad = jnp.mean(grad_unit, axis=-1, keepdims=True)
    mean_proj = jnp.mean(grad_unit * unit_rows, axis=-1, keepdims=True)
    d_tokens = (grad_f32 + inv_std * (grad_unit - mean_grad - unit_rows * mean_proj)).astype(
        jnp.bfloat16
    )
    shares = (
        lax.psum_scatter(
            d_w_qkv.astype(jnp.bfloat16), "narrow", scatter_dimension=1, tiled=True
        ).astype(jnp.float32),
        lax.psum_scatter(
            d_b_qkv.astype(jnp.bfloat16), "narrow", scatter_dimension=0, tiled=True
        ).astype(jnp.float32),
        lax.psum_scatter(
            d_w_dense.astype(jnp.bfloat16), "narrow", scatter_dimension=0, tiled=True
        ).astype(jnp.float32),
        lax.psum_scatter(
            d_out_bias.astype(jnp.bfloat16), "narrow", scatter_dimension=0, tiled=True
        ).astype(jnp.float32),
        lax.psum_scatter(
            d_ln_gain.astype(jnp.bfloat16), "narrow", scatter_dimension=0, tiled=True
        ).astype(jnp.float32),
        lax.psum_scatter(
            d_ln_bias.astype(jnp.bfloat16), "narrow", scatter_dimension=0, tiled=True
        ).astype(jnp.float32),
    )
    d_w_qkv, d_b_qkv, d_w_dense, d_out_bias, d_ln_gain, d_ln_bias = shares
    summed = lax.psum(
        (d_w_qkv, d_b_qkv, d_w_dense, d_out_bias, d_ln_gain, d_ln_bias, d_w_up, d_b_up, d_w_down),
        "wide",
    )
    d_w_qkv, d_b_qkv, d_w_dense, d_out_bias, d_ln_gain, d_ln_bias, d_w_up, d_b_up, d_w_down = summed
    return (
        mixed,
        d_tokens,
        d_ln_gain,
        d_ln_bias,
        d_w_qkv,
        d_b_qkv,
        d_w_dense,
        d_w_up,
        d_b_up,
        d_w_down,
        d_out_bias,
    )


def solution(mesh):
    in_specs = (
        P(("wide", "narrow"), None),
        P(("wide", "narrow"), None),
        P(),
        P(),
        P(),
        P(),
        P(),
        P(None, "narrow"),
        P("narrow"),
        P("narrow", None),
        P(),
        P(("wide", "narrow"), None),
    )
    out_specs = (
        P(("wide", "narrow"), None),
        P(("wide", "narrow"), None),
        P("narrow"),
        P("narrow"),
        P(None, "narrow"),
        P("narrow"),
        P("narrow", None),
        P(None, "narrow"),
        P("narrow"),
        P("narrow", None),
        P("narrow"),
    )
    return jax.shard_map(body, mesh=mesh, in_specs=in_specs, out_specs=out_specs, check_vma=False)
```

```python
import functools
import math

import jax
import jax.numpy as jnp
from jax import lax
from jax.experimental import pallas as pl
from jax.experimental.pallas import tpu as pltpu
from jax.sharding import PartitionSpec as P

D = 1024
HEADS = 16
HEAD = 64
ROT = 16


TILE = 256
PAIR = 2 * HEAD
MAX_DOC = 512


def doc_starts(segments):
    return jnp.sum((segments[:, :, None] > segments[:, None, :]).astype(jnp.int32), axis=2)


def rope_coefs(position):
    half_rot = ROT // 2
    lane = jnp.arange(PAIR, dtype=jnp.int32) % HEAD
    inv_freq = 1.0 / 10000.0 ** ((lane % half_rot).astype(jnp.float32) * 2.0 / ROT)
    angles = position.astype(jnp.float32)[:, None] * inv_freq[None, :]
    cos, sin = jnp.cos(angles), jnp.sin(angles)
    rotated = (lane < ROT)[None, :]
    first = (lane < half_rot)[None, :]
    return (
        jnp.where(rotated, cos, 1.0),
        jnp.where(first, -sin, 0.0),
        jnp.where(rotated & ~first, sin, 0.0),
    )


def turn(t, same, down, up):
    half_rot = ROT // 2
    return (
        t * same
        + pltpu.roll(t, PAIR - half_rot, axis=1) * down
        + pltpu.roll(t, half_rot, axis=1) * up
    )


def dot_nt(left, right):
    return lax.dot_general(
        left, right, (((1,), (1,)), ((), ())), preferred_element_type=jnp.float32
    )


def dot_nn(left, right):
    return lax.dot_general(
        left, right, (((1,), (0,)), ((), ())), preferred_element_type=jnp.float32
    )


def qkv_kernel(
    x_ref, gain_ref, bias_ref, w_ref, b_ref, same_ref, down_ref, up_ref, out_ref, normed_ref, turned_ref
):
    step = pl.program_id(0)
    rows, cols = out_ref.shape
    blocks = (HEADS * HEAD) // cols

    @pl.when(step == 0)
    def _():
        for r in range(0, rows, TILE):
            x = x_ref[r : r + TILE, :].astype(jnp.float32)
            mean = jnp.mean(x, axis=-1, keepdims=True)
            centered = x - mean
            variance = jnp.mean(centered * centered, axis=-1, keepdims=True)
            unit = centered * lax.rsqrt(variance + 1e-05)
            normed = unit * gain_ref[...] + bias_ref[...]
            normed_ref[r : r + TILE, :] = normed.astype(jnp.bfloat16)
            turned_ref[:, r : r + TILE] = normed.T.astype(jnp.bfloat16)

    scale = jnp.where(step < blocks, 1.0 / math.sqrt(HEAD), 1.0)
    for r in range(0, rows, TILE):
        acc = dot_nn(normed_ref[r : r + TILE, :], w_ref[...]) + b_ref[...]

        @pl.when(step < 2 * blocks)
        def _():
            same = same_ref[r : r + TILE, :]
            down = down_ref[r : r + TILE, :]
            up = up_ref[r : r + TILE, :]
            for c in range(0, cols, PAIR):
                out_ref[r : r + TILE, c : c + PAIR] = (
                    turn(acc[:, c : c + PAIR], same, down, up) * scale
                ).astype(jnp.bfloat16)

        @pl.when(step >= 2 * blocks)
        def _():
            out_ref[r : r + TILE, :] = acc.astype(jnp.bfloat16)


def project(tokens, gain, bias, w_qkv, b_qkv, coefs):
    rows, width = tokens.shape
    cols = 512
    whole = lambda shape: pl.BlockSpec(shape, lambda j: (0, 0))
    return pl.pallas_call(
        qkv_kernel,
        grid=(w_qkv.shape[1] // cols,),
        in_specs=[
            whole((rows, width)),
            whole((1, width)),
            whole((1, width)),
            pl.BlockSpec((width, cols), lambda j: (0, j)),
            pl.BlockSpec((1, cols), lambda j: (0, j)),
            whole((rows, PAIR)),
            whole((rows, PAIR)),
            whole((rows, PAIR)),
        ],
        out_specs=[pl.BlockSpec((rows, cols), lambda j: (0, j)), whole((rows, width)), whole((width, rows))],
        out_shape=[
            jax.ShapeDtypeStruct((rows, w_qkv.shape[1]), jnp.bfloat16),
            jax.ShapeDtypeStruct((rows, width), jnp.bfloat16),
            jax.ShapeDtypeStruct((width, rows), jnp.bfloat16),
        ],
        compiler_params=pltpu.CompilerParams(vmem_limit_bytes=60 << 20),
        cost_estimate=pl.CostEstimate(
            flops=2 * rows * width * w_qkv.shape[1],
            bytes_accessed=2 * (rows * width * 2 + width * w_qkv.shape[1] * 2),
            transcendentals=0,
        ),
    )(tokens, gain, bias, w_qkv, b_qkv, *coefs)


def attention_kernel(
    first_ref,
    start_ref,
    q_ref,
    k_ref,
    v_ref,
    g_ref,
    same_ref,
    down_ref,
    up_ref,
    att_ref,
    grad_ref,
    dk_acc,
    dv_acc,
    kt_ref,
    vt_ref,
):
    rows = q_ref.shape[0]
    lane = lax.broadcasted_iota(jnp.int32, (1, PAIR), 1)
    dk_acc[...] = jnp.zeros_like(dk_acc)
    dv_acc[...] = jnp.zeros_like(dv_acc)
    kt_ref[...] = k_ref[...].astype(jnp.float32).T.astype(jnp.bfloat16)
    vt_ref[...] = v_ref[...].astype(jnp.float32).T.astype(jnp.bfloat16)

    def one_block(block, first, count):
        at = pl.multiple_of(block * TILE, TILE)
        here = pl.ds(at, TILE)
        q_pair, g_pair = q_ref[here, :], g_ref[here, :]
        start = start_ref[:, here]
        query_index = at + lax.broadcasted_iota(jnp.int32, (1, TILE), 1)
        keys = [
            pl.ds(pl.multiple_of((first + j) * TILE, TILE), TILE) for j in range(count)
        ]
        key_index = [
            (first + j) * TILE + lax.broadcasted_iota(jnp.int32, (TILE, TILE), 0)
            for j in range(count)
        ]
        visible = [(idx >= start) & (idx <= query_index) for idx in key_index]
        out_t, dq_t = [], []
        for head in range(2):
            mine = (lane >= head * HEAD) & (lane < (head + 1) * HEAD)
            q = jnp.where(mine, q_pair, jnp.zeros_like(q_pair))
            g = jnp.where(mine, g_pair, jnp.zeros_like(g_pair))
            wide = slice(head * HEAD, (head + 1) * HEAD)
            scores = [
                jnp.where(visible[j], dot_nt(k_ref[keys[j], :], q), -1e30) for j in range(count)
            ]
            grad_prob = [dot_nt(v_ref[keys[j], :], g) for j in range(count)]
            top = jnp.max(scores[0], axis=0, keepdims=True)
            for j in range(1, count):
                top = jnp.maximum(top, jnp.max(scores[j], axis=0, keepdims=True))
            exps = [jnp.exp(s - top) for s in scores]
            total = sum(jnp.sum(e, axis=0, keepdims=True) for e in exps)
            inverse = 1.0 / total
            probs = [e * inverse for e in exps]
            row_dot = sum(
                jnp.sum(p * d, axis=0, keepdims=True) for p, d in zip(probs, grad_prob)
            )
            out_head = jnp.zeros((HEAD, TILE), jnp.float32)
            dq_head = jnp.zeros((HEAD, TILE), jnp.float32)
            for j in range(count):
                low = probs[j].astype(jnp.bfloat16)
                grad_score = (probs[j] * (grad_prob[j] - row_dot)).astype(jnp.bfloat16)
                out_head += dot_nn(vt_ref[wide, keys[j]], low)
                dq_head += dot_nn(kt_ref[wide, keys[j]], grad_score)
                dv_acc[keys[j], :] += dot_nn(low, g)
                dk_acc[keys[j], :] += dot_nn(grad_score, q)
            out_t.append(out_head)
            dq_t.append(dq_head)
        att_ref[here, :] = jnp.concatenate(out_t, axis=0).T.astype(jnp.bfloat16)
        dq = jnp.concatenate(dq_t, axis=0).T * (1.0 / math.sqrt(HEAD))
        grad_ref[0, here, :] = turn(
            dq, same_ref[here, :], -down_ref[here, :], -up_ref[here, :]
        ).astype(jnp.bfloat16)

    span = MAX_DOC // TILE + 1

    def step(block, carry):
        first = first_ref[block]
        count = block + 1 - first
        for n in range(1, span + 1):

            @pl.when(count == n)
            def _(n=n):
                one_block(block, first, n)

        return carry

    lax.fori_loop(0, rows // TILE, step, 0)
    grad_ref[1] = turn(dk_acc[...], same_ref[...], -down_ref[...], -up_ref[...]).astype(
        jnp.bfloat16
    )
    grad_ref[2] = dv_acc[...].astype(jnp.bfloat16)


def attend(qkv, grad_att, starts, coefs):
    rows = qkv.shape[0]
    width = HEADS * HEAD
    pairs = width // PAIR
    first = starts[::TILE] // TILE
    whole = pl.BlockSpec((rows, PAIR), lambda i, f: (0, 0))
    return pl.pallas_call(
        attention_kernel,
        grid_spec=pltpu.PrefetchScalarGridSpec(
            num_scalar_prefetch=1,
            grid=(pairs,),
            in_specs=[
                pl.BlockSpec((1, rows), lambda i, f: (0, 0)),
                pl.BlockSpec((rows, PAIR), lambda i, f: (0, i)),
                pl.BlockSpec((rows, PAIR), lambda i, f: (0, pairs + i)),
                pl.BlockSpec((rows, PAIR), lambda i, f: (0, 2 * pairs + i)),
                pl.BlockSpec((rows, PAIR), lambda i, f: (0, i)),
                whole,
                whole,
                whole,
            ],
            out_specs=[
                pl.BlockSpec((rows, PAIR), lambda i, f: (0, i)),
                pl.BlockSpec((3, rows, PAIR), lambda i, f: (0, 0, i)),
            ],
            scratch_shapes=[
                pltpu.VMEM((rows, PAIR), jnp.float32),
                pltpu.VMEM((rows, PAIR), jnp.float32),
                pltpu.VMEM((PAIR, rows), jnp.bfloat16),
                pltpu.VMEM((PAIR, rows), jnp.bfloat16),
            ],
        ),
        out_shape=[
            jax.ShapeDtypeStruct((rows, width), jnp.bfloat16),
            jax.ShapeDtypeStruct((3, rows, width), jnp.bfloat16),
        ],
        compiler_params=pltpu.CompilerParams(vmem_limit_bytes=60 << 20),
        cost_estimate=pl.CostEstimate(
            flops=16 * rows * rows * width, bytes_accessed=16 * rows * width, transcendentals=0
        ),
    )(first, starts[None, :], qkv, qkv, qkv, grad_att, *coefs)


CORE, YAXIS, XHALF, NEAR, BACK, WIDE_A, WIDE_B, FAR = range(8)
BLOCKS, QKV, DENSE = 12, 3, 3
F_RING, Y_RING, S_RING = 8, 4, 2
PACK = 2 * TILE + 16
LAGS = (2, 3, 4, 5, 6, 7)
MESH = pl.DeviceIdType.MESH


def xor2(value, other):
    return (value + other) % 2 + 2 * ((value // 2 + other // 2) % 2)


def gelu_parts(x):
    cdf = 0.5 * (1.0 + lax.erf(x * math.sqrt(0.5)))
    density = jnp.exp(-0.5 * x * x) * (1.0 / math.sqrt(2.0 * math.pi))
    return x * cdf, cdf + x * density


def widen(value):
    return value.astype(jnp.float32)


def main_kernel(
    wide,
    tokens,
    normed,
    normed_t,
    cot,
    attended,
    gp,
    w_qkv,
    w_dense,
    own_w,
    y_w,
    gain,
    out_bias,
    mixed_out,
    dtok_out,
    straight_out,
    turned_out,
    small_out,
    core_w,
    diag_w,
    nrm,
    nrm_t,
    ct,
    ct_t,
    hid,
    gpre,
    pool,
    mixed_acc,
    gn_acc,
    slope,
    s_ring,
    a_ring,
    f_ring,
    r_ring,
    ry,
    rx,
    rz,
    rfar,
    gz,
    gx,
    tbuf,
    bias,
    sv,
    sv_sum,
    sv_recv,
    send,
    recv,
    far_send,
    far_recv,
    sv_send,
    sv_rsem,
    load,
    load_w,
    out_sem,
    w_send,
    w_recv,
    free,
    y_free,
):
    rows = nrm.shape[0]
    R_RING, A_RING = r_ring.shape[1], a_ring.shape[0]
    n, w = lax.axis_index("narrow"), lax.axis_index("wide")
    near = w % 4
    xbit, zbit = w % 2, (w // 2) % 2
    bits = [b for b in range(2, 20) if (1 << b) < wide]
    mate = {"narrow": n + 1 - 2 * (n % 2)}
    ymate = {"narrow": n + 2 - 4 * (n // 2)}

    def across(bit):
        return {"wide": w + (1 << bit) - (2 << bit) * ((w // (1 << bit)) % 2)}

    def spot(r):
        return xor2(n, r)

    partners = [mate, ymate] + [across(b) for b in [0, 1] + bits]
    barrier = pltpu.get_barrier_semaphore()
    for p in partners:
        pl.semaphore_signal(barrier, inc=1, device_id=p, device_id_type=MESH)
    pl.semaphore_wait(barrier, len(partners))

    half, quarter = rows // 2, rows // 4
    own_half, other_half = half * xbit, half * (1 - xbit)
    own_q = own_half + quarter * zbit
    other_q = own_half + quarter * (1 - zbit)

    def seg(start, size):
        return pl.ds(pl.multiple_of(start, quarter), size)

    def remote(src, dst, kind, b, dev):
        return pltpu.make_async_remote_copy(
            src_ref=src,
            dst_ref=dst,
            send_sem=send.at[kind, b],
            recv_sem=recv.at[kind, b],
            device_id=dev,
            device_id_type=MESH,
        )

    def core_copy(which, b):
        return remote(
            s_ring.at[which, b % S_RING],
            r_ring.at[which, b % R_RING],
            CORE if which == 0 else BACK,
            b,
            mate,
        )

    def y_copy(b):
        return remote(a_ring.at[b % A_RING], ry.at[b % Y_RING], YAXIS, b, ymate)

    def x_copy(b):
        return remote(f_ring.at[b % F_RING, seg(other_half, half)], rx.at[b], XHALF, b, across(0))

    def z_copy(b):
        return remote(f_ring.at[b % F_RING, seg(other_q, quarter)], rz.at[b], NEAR, b, across(1))

    def far_copy(i, b):
        return pltpu.make_async_remote_copy(
            src_ref=f_ring.at[b % F_RING, seg(own_q, quarter)],
            dst_ref=rfar.at[i, b],
            send_sem=far_send.at[i, b],
            recv_sem=far_recv.at[i, b],
            device_id=across(bits[i]),
            device_id_type=MESH,
        )

    def back_z(b):
        return remote(f_ring.at[b % F_RING, seg(own_q, quarter)], gz.at[b], FAR, b, across(1))

    def back_xa(b):
        return remote(
            f_ring.at[b % F_RING, seg(own_q, quarter)], gx.at[b, 0], WIDE_A, b, across(0)
        )

    def back_xb(b):
        return remote(gz.at[b], gx.at[b, 1], WIDE_B, b, across(0))

    def is_turned(b):
        return (b == DENSE) | ((b > DENSE) & (b % 2 == 0))

    def piece(i, b):
        src = (
            f_ring.at[b % F_RING, seg(own_q, quarter)],
            gz.at[b],
            gx.at[b, 0],
            gx.at[b, 1],
        )[i]
        at = own_half if i < 2 else other_half
        return src, at + quarter * (zbit if i % 2 == 0 else 1 - zbit)

    def straight_copy(i, b):
        src, at = piece(i, b)
        column = jnp.where(b < QKV, b, QKV + (b - DENSE - 2) // 2)
        column = pl.ds(pl.multiple_of(column * TILE, TILE), TILE)
        return pltpu.make_async_copy(
            src, straight_out.at[seg(at, quarter), column], out_sem.at[i, b]
        )

    def turned_copy(i, b):
        src, at = piece(i, b)
        row = jnp.where(b == DENSE, 0, 1 + (b - DENSE - 1) // 2)
        return pltpu.make_async_copy(
            tbuf.at[(b // 2) % 2, i],
            turned_out.at[pl.ds(pl.multiple_of(row * TILE, TILE), TILE), seg(at, quarter)],
            out_sem.at[i, b],
        )

    def put(i, b):
        @pl.when(is_turned(b))
        def _():
            src, at = piece(i, b)
            tbuf[(b // 2) % 2, i] = widen(src[...]).T.astype(jnp.bfloat16)
            turned_copy(i, b).start()

        @pl.when(jnp.logical_not(is_turned(b)))
        def _():
            straight_copy(i, b).start()

    def add_into(b, start, size, other):
        at = seg(start, size)
        slot = b % F_RING
        f_ring[slot, at] = (widen(f_ring[slot, at]) + widen(other[...])).astype(jnp.bfloat16)

    def stage_y(b):
        y_copy(b).wait_recv()
        add_into(b, other_half, half, ry.at[b % Y_RING, seg(other_half, half)])
        x_copy(b).start()
        add_into(b, own_half, half, ry.at[b % Y_RING, seg(own_half, half)])

        @pl.when(b + Y_RING < BLOCKS)
        def _():
            pl.semaphore_signal(y_free, inc=1, device_id=ymate, device_id_type=MESH)

    def stage_x(b):
        x_copy(b).wait_recv()
        add_into(b, other_q, quarter, rx.at[b, seg(quarter * (1 - zbit), quarter)])
        z_copy(b).start()
        add_into(b, own_q, quarter, rx.at[b, seg(quarter * zbit, quarter)])

    def stage_near(b):
        z_copy(b).wait_recv()
        add_into(b, own_q, quarter, rz.at[b])
        far_copy(0, b).start()

    def stage_far(b):
        for i in range(len(bits)):
            far_copy(i, b).wait()
            add_into(b, own_q, quarter, rfar.at[i, b])
            if i + 1 < len(bits):
                far_copy(i + 1, b).start()
        back_z(b).start()
        back_xa(b).start()
        put(0, b)
        x_copy(b).wait_send()
        z_copy(b).wait_send()

    def stage_back(b):
        back_z(b).wait_recv()
        back_xb(b).start()
        put(1, b)

    def stage_out(b):
        back_xa(b).wait_recv()
        put(2, b)
        back_xb(b).wait_recv()
        put(3, b)
        back_z(b).wait_send()
        back_xa(b).wait_send()
        back_xb(b).wait_send()
        for i in range(4):
            straight_copy(i, b).wait()

    stages = (stage_y, stage_x, stage_near, stage_far, stage_back, stage_out)

    def progress(t):
        for lag, stage in reversed(list(zip(LAGS, stages))):
            b = t - lag

            @pl.when((b >= 0) & (b < BLOCKS))
            def _(stage=stage, b=b):
                stage(b)

    step = rows // 2

    def tile(r, b, left, right):
        if r in (1, 3):
            which = r // 2

            @pl.when(b >= S_RING)
            def _():
                core_copy(which, b - S_RING).wait_send()

            def chunk(m, c):
                at = pl.ds(pl.multiple_of(m * step, step), step)
                s_ring[which, b % S_RING, at] = dot_nn(left[at, :], right[...]).astype(jnp.bfloat16)
                return c

            lax.fori_loop(0, 2, chunk, 0)
            if which == 0:

                @pl.when(b >= R_RING)
                def _():
                    pl.semaphore_wait(free, 1)

            core_copy(which, b).start()
        else:
            which = 1 if r == 2 else 0
            if r == 2:

                @pl.when(b >= A_RING)
                def _():
                    y_copy(b - A_RING).wait_send()

            core_copy(which, b).wait_recv()
            target = a_ring.at[b % A_RING] if r == 2 else f_ring.at[b % F_RING]

            def chunk(m, c):
                at = pl.ds(pl.multiple_of(m * step, step), step)
                target[at] = (
                    dot_nn(left[at, :], right[...]) + widen(r_ring[which, b % R_RING, at])
                ).astype(jnp.bfloat16)
                return c

            lax.fori_loop(0, 2, chunk, 0)
            if r == 2:

                @pl.when(b >= Y_RING)
                def _():
                    pl.semaphore_wait(y_free, 1)

                y_copy(b).start()
            else:

                @pl.when(b + R_RING < BLOCKS)
                def _():
                    pl.semaphore_signal(free, inc=1, device_id=mate, device_id_type=MESH)

    def accumulate(target, left, right, transposed, first):
        size = rows // 4

        def chunk(m, c):
            at = pl.ds(pl.multiple_of(m * size, size), size)
            dot = dot_nt if transposed else dot_nn
            got = dot(left[at, :], right[...])
            target[at, :] = got if first else target[at, :] + got
            return c

        lax.fori_loop(0, 4, chunk, 0)

    def weight_copy(k, at):
        return pltpu.make_async_remote_copy(
            src_ref=(own_w, y_w)[k].at[at],
            dst_ref=(core_w, diag_w)[k].at[at],
            send_sem=w_send.at[k, at],
            recv_sem=w_recv.at[k, at],
            device_id=mate,
            device_id_type=MESH,
        )

    firsts = [
        pltpu.make_async_copy(normed_t, nrm_t, load.at[0]),
        pltpu.make_async_copy(cot, ct, load.at[1]),
        pltpu.make_async_copy(attended, hid, load.at[2]),
        pltpu.make_async_copy(w_dense, gpre, load.at[3]),
        pltpu.make_async_copy(normed, nrm, load.at[4]),
    ]
    firsts[0].start()

    def gp_tile(r, j):
        at = 3 * spot(r) + j
        return pltpu.make_async_copy(
            gp.at[at // 4, :, pl.ds(pl.multiple_of((at % 4) * TILE, TILE), TILE)],
            pool.at[j % 2, :, r * TILE : (r + 1) * TILE],
            load_w.at[j % 2, r],
        )

    def chunk_copies(c):
        return [
            pltpu.make_async_copy(gp.at[c], pool.at[2], load.at[6]),
            pltpu.make_async_copy(
                w_qkv.at[:, pl.ds(pl.multiple_of(c * rows, rows), rows)], pool.at[3], load.at[7]
            ),
        ]

    for r in (1, 3, 2, 0):
        gp_tile(r, 0).start()
    for c in firsts[1:]:
        c.start()
    for c in chunk_copies(0):
        c.start()
    sv[...] = jnp.zeros_like(sv)
    firsts[0].wait()

    def qkv_block(j, carry):
        @pl.when(j + 1 < QKV)
        def _():
            for r in (1, 3, 2, 0):
                gp_tile(r, j + 1).start()

        for r in (1, 3, 2, 0):
            gp_tile(r, j).wait()
            mine = pool.at[j % 2, :, r * TILE : (r + 1) * TILE]
            tile(r, j, nrm_t, mine)
            sv[r, pl.ds(3 + j, 1), :] = jnp.sum(widen(mine[...]), axis=0, keepdims=True)

        @pl.when(j == 0)
        def _():
            for at in range(4):
                weight_copy(0, at).start()
                weight_copy(1, at).start()
            firsts[1].wait()
            for at in range(0, rows, TILE):
                ct_t[:, at : at + TILE] = widen(ct[at : at + TILE, :]).T.astype(jnp.bfloat16)

        for c in chunk_copies(j):
            c.wait()

        @pl.when(j == 0)
        def _():
            accumulate(gn_acc, pool.at[2], pool.at[3], True, True)

        @pl.when(j > 0)
        def _():
            accumulate(gn_acc, pool.at[2], pool.at[3], True, False)

        @pl.when(j + 1 < QKV)
        def _():
            for c in chunk_copies(j + 1):
                c.start()

        progress(j)
        return carry

    lax.fori_loop(0, QKV, qkv_block, 0)

    for c in firsts[2:]:
        c.wait()
    for r in (1, 3, 2, 0):
        at = pl.ds(pl.multiple_of(spot(r) * TILE, TILE), TILE)
        tile(r, DENSE, ct_t, hid.at[:, at])
    accumulate(mixed_acc, hid, gpre, False, True)
    progress(DENSE)

    def weights(cb):
        slot = cb % 2
        far = xor2(cb, near)
        copies = []
        for r, src in enumerate((own_w.at[cb], core_w.at[cb], y_w.at[far], diag_w.at[far])):
            copies.append(
                pltpu.make_async_copy(
                    src.at[2 * TILE : PACK], bias.at[slot, r], load_w.at[2 + slot, 8 + r]
                )
            )
            for k in range(2):
                copies.append(
                    pltpu.make_async_copy(
                        src.at[k * TILE : (k + 1) * TILE],
                        pool.at[2 * slot + k, r * TILE : (r + 1) * TILE],
                        load_w.at[2 + slot, 2 * r + k],
                    )
                )
        return copies

    def weights_here(cb):
        weight_copy(0, cb).wait_recv()
        weight_copy(1, xor2(cb, near)).wait_recv()
        for c in weights(cb):
            c.start()

    weights_here(0)

    def mlp_block(cb, carry):
        slot = cb % 2

        @pl.when(cb < 3)
        def _():
            weights_here(cb + 1)

        for c in weights(cb):
            c.wait()
        for r in (1, 3, 2, 0):
            cols = slice(r * TILE, (r + 1) * TILE)
            up, down = pool.at[2 * slot, cols], pool.at[2 * slot + 1, cols]

            bias_row = widen(bias[slot, r, 0:1, 0:TILE])

            def act(m, c):
                at = pl.ds(pl.multiple_of(m * TILE, TILE), TILE)
                pre = dot_nt(nrm[at, :], up[...]) + bias_row
                value, grad = gelu_parts(pre)
                hid[at, cols] = value.astype(jnp.bfloat16)
                slope[at, :] = grad
                return c

            lax.fori_loop(0, rows // TILE, act, 0)
            tile(r, 4 + 2 * cb, ct_t, hid.at[:, cols])

            def back(m, total):
                at = pl.ds(pl.multiple_of(m * TILE, TILE), TILE)
                low = (dot_nt(ct[at, :], down[...]) * slope[at, :]).astype(jnp.bfloat16)
                gpre[at, cols] = low
                return total + jnp.sum(widen(low), axis=0, keepdims=True)

            total = lax.fori_loop(0, rows // TILE, back, jnp.zeros((1, TILE), jnp.float32))
            sv[r, pl.ds(6 + cb, 1), :] = total
            if r == 0:
                progress(4 + 2 * cb)
            tile(r, 5 + 2 * cb, nrm_t, gpre.at[:, cols])
        accumulate(mixed_acc, hid, pool.at[2 * slot + 1], False, False)
        accumulate(gn_acc, gpre, pool.at[2 * slot], False, False)
        progress(5 + 2 * cb)
        return carry

    lax.fori_loop(0, 4, mlp_block, 0)

    tok_load = pltpu.make_async_copy(tokens, pool.at[0], load.at[0])
    tok_load.start()
    progress(BLOCKS)
    tok_load.wait()

    def finish(m, sums):
        at = pl.ds(pl.multiple_of(m * TILE, TILE), TILE)
        x = widen(pool[0, at, :])
        mean = jnp.mean(x, axis=-1, keepdims=True)
        centered = x - mean
        variance = jnp.mean(centered * centered, axis=-1, keepdims=True)
        inv_std = lax.rsqrt(variance + 1e-05)
        unit = centered * inv_std
        hid[at, :] = (mixed_acc[at, :] + x + out_bias[...]).astype(jnp.bfloat16)
        gn = gn_acc[at, :]
        g = gn * gain[...]
        mean_grad = jnp.mean(g, axis=-1, keepdims=True)
        mean_proj = jnp.mean(g * unit, axis=-1, keepdims=True)
        c = widen(ct[at, :])
        gpre[at, :] = (c + inv_std * (g - mean_grad - unit * mean_proj)).astype(jnp.bfloat16)
        return (
            sums[0] + jnp.sum(gn * unit, axis=0, keepdims=True),
            sums[1] + jnp.sum(gn, axis=0, keepdims=True),
            sums[2] + jnp.sum(c, axis=0, keepdims=True),
        )

    zero = jnp.zeros((1, rows), jnp.float32)
    sums = lax.fori_loop(0, rows // TILE, finish, (zero, zero, zero))
    final = [
        pltpu.make_async_copy(hid, mixed_out, load.at[1]),
        pltpu.make_async_copy(gpre, dtok_out, load.at[2]),
    ]
    for c in final:
        c.start()
    for i in range(3):
        sv_sum[i : i + 1, :] = sums[i]
    for r in range(4):
        at = pl.ds(pl.multiple_of(spot(r) * TILE, TILE), TILE)
        sv[r, 0:3, :] = sv_sum[0:3, at]

    def sv_copy(i, src, dev):
        return pltpu.make_async_remote_copy(
            src_ref=src,
            dst_ref=sv_recv.at[i],
            send_sem=sv_send.at[i],
            recv_sem=sv_rsem.at[i],
            device_id=dev,
            device_id_type=MESH,
        )

    hops = [
        sv_copy(0, sv.at[1], mate),
        sv_copy(1, sv.at[3], mate),
        sv_copy(2, sv.at[2], ymate),
    ]
    hops += [sv_copy(3 + i, sv.at[0], across(b)) for i, b in enumerate([0, 1] + bits)]
    hops[0].start()
    hops[1].start()
    progress(BLOCKS + 1)
    hops[0].wait()
    hops[1].wait()
    sv[0] = sv[0] + sv_recv[0]
    sv[2] = sv[2] + sv_recv[1]
    hops[2].start()
    progress(BLOCKS + 2)
    hops[2].wait()
    sv[0] = sv[0] + sv_recv[2]
    for i in range(3, len(hops)):
        hops[i].start()
        if i < 6:
            progress(BLOCKS + i)
        hops[i].wait()
        sv[0] = sv[0] + sv_recv[i]
    for i in range(len(hops), 6):
        progress(BLOCKS + i)
    small_out[...] = sv[0]
    progress(BLOCKS + 6)

    for at in range(4):
        weight_copy(0, at).wait_send()
        weight_copy(1, at).wait_send()
    for c in final:
        c.wait()
    for b in range(BLOCKS - S_RING, BLOCKS):
        core_copy(0, b).wait_send()
        core_copy(1, b).wait_send()
    for b in range(BLOCKS - A_RING, BLOCKS):
        y_copy(b).wait_send()


def main_call(wide, hbm_args, vmem_args):
    tokens = hbm_args[0]
    rows, width = tokens.shape
    hops = max(wide.bit_length() - 1, 2)
    far = hops - 2
    bf, f32 = jnp.bfloat16, jnp.float32
    half, quarter = rows // 2, rows // 4
    vm = pltpu.VMEM
    dma = pltpu.SemaphoreType.DMA
    return pl.pallas_call(
        functools.partial(main_kernel, wide),
        in_specs=[pl.BlockSpec(memory_space=pl.ANY)] * len(hbm_args)
        + [pl.BlockSpec(memory_space=pltpu.VMEM)] * len(vmem_args),
        out_specs=[pl.BlockSpec(memory_space=pl.ANY)] * 4
        + [pl.BlockSpec(memory_space=pltpu.VMEM)]
        + [pl.BlockSpec(memory_space=pl.ANY)] * 2,
        out_shape=[
            jax.ShapeDtypeStruct((rows, width), bf),
            jax.ShapeDtypeStruct((rows, width), bf),
            jax.ShapeDtypeStruct((width, 7 * TILE), bf),
            jax.ShapeDtypeStruct((5 * TILE, width), bf),
            jax.ShapeDtypeStruct((16, TILE), f32),
            jax.ShapeDtypeStruct((4, PACK, width), bf),
            jax.ShapeDtypeStruct((4, PACK, width), bf),
        ],
        scratch_shapes=[
            vm((rows, width), bf),
            vm((width, rows), bf),
            vm((rows, width), bf),
            vm((width, rows), bf),
            vm((rows, width), bf),
            vm((rows, width), bf),
            vm((4, rows, width), bf),
            vm((rows, width), f32),
            vm((rows, width), f32),
            vm((rows, TILE), f32),
            vm((2, S_RING, width, TILE), bf),
            vm((4 if far < 2 else 2, width, TILE), bf),
            vm((F_RING, width, TILE), bf),
            vm((2, 4 if far < 2 else 2, width, TILE), bf),
            vm((Y_RING, width, TILE), bf),
            vm((BLOCKS, half, TILE), bf),
            vm((BLOCKS, quarter, TILE), bf),
            vm((far, BLOCKS, quarter, TILE), bf),
            vm((BLOCKS, quarter, TILE), bf),
            vm((BLOCKS, 2, quarter, TILE), bf),
            vm((2, 4, TILE, TILE), bf),
            vm((2, 4, 16, width), bf),
            vm((4, 16, TILE), f32),
            vm((8, width), f32),
            vm((3 + hops, 16, TILE), f32),
            dma((8, BLOCKS)),
            dma((8, BLOCKS)),
            dma((far, BLOCKS)),
            dma((far, BLOCKS)),
            dma((3 + hops,)),
            dma((3 + hops,)),
            dma((8,)),
            dma((4, 12)),
            dma((4, BLOCKS)),
            dma((2, 4)),
            dma((2, 4)),
            pltpu.SemaphoreType.REGULAR,
            pltpu.SemaphoreType.REGULAR,
        ],
        compiler_params=pltpu.CompilerParams(
            collective_id=0, has_side_effects=True, vmem_limit_bytes=61 << 20
        ),
        cost_estimate=pl.CostEstimate(
            flops=70 * rows * width * width, bytes_accessed=80 << 20, transcendentals=0
        ),
    )(*hbm_args, *vmem_args)


def flip(value, axis, bit, size):
    return lax.ppermute(value, axis, [(i, i ^ bit) for i in range(size)])


def make_body(wide):
    def body(
        tokens,
        seg_ids,
        ln_gain,
        ln_bias,
        w_qkv,
        b_qkv,
        w_dense,
        w_up,
        b_up,
        w_down,
        out_bias,
        cotangent,
    ):
        seq_len = seg_ids.shape[1]
        width = tokens.shape[1]
        index = lax.axis_index("wide")
        near = index % 4

        pad = jnp.zeros((4, 16, width - TILE), jnp.bfloat16)
        b_rows = jnp.broadcast_to(b_up.reshape(4, 1, TILE), (4, 16, TILE))
        own_w = jnp.concatenate(
            [
                w_up.T.reshape(4, TILE, width),
                w_down.reshape(4, TILE, width),
                jnp.concatenate([b_rows, pad], axis=2),
            ],
            axis=1,
        )
        across_y = flip(
            lax.dynamic_index_in_dim(own_w, near, 0, keepdims=False), "narrow", 2, 4
        )

        starts = doc_starts(seg_ids)
        position = jnp.arange(seq_len, dtype=jnp.int32)[None, :] - starts
        coefs = rope_coefs(position[0])
        gain = ln_gain.astype(jnp.float32)[None, :]
        grad_att = dot_nt(cotangent, w_dense).astype(jnp.bfloat16)
        qkv, normed, normed_t = project(
            tokens,
            gain,
            ln_bias.astype(jnp.float32)[None, :],
            w_qkv,
            b_qkv.astype(jnp.float32)[None, :],
            coefs,
        )
        across_y, qkv, grad_att = lax.optimization_barrier((across_y, qkv, grad_att))
        others = [flip(across_y, "wide", k, wide) for k in (1, 2, 3)]
        attended, grad_proj = attend(qkv, grad_att, starts[0], coefs)
        others, attended = lax.optimization_barrier((others, attended))
        y_w = jnp.stack([across_y] + others, axis=0)
        mixed, d_tokens, straight, turned, small, _, _ = main_call(
            wide,
            (
                tokens,
                normed,
                normed_t,
                cotangent,
                attended,
                grad_proj,
                w_qkv,
                w_dense,
                own_w,
                y_w,
            ),
            (gain, out_bias.astype(jnp.float32)[None, :]),
        )
        q = QKV * TILE
        d_w_qkv = straight[:, :q].astype(jnp.float32)
        d_w_up = straight[:, q:].astype(jnp.float32)
        d_w_dense = turned[:TILE].astype(jnp.float32)
        d_w_down = turned[TILE:].astype(jnp.float32)
        return (
            mixed,
            d_tokens,
            small[0],
            small[1],
            d_w_qkv,
            small[3:6].reshape(-1),
            d_w_dense,
            d_w_up,
            small[6:10].reshape(-1),
            d_w_down,
            small[2],
        )

    return body


def solution(mesh):
    in_specs = (
        P(("wide", "narrow"), None),
        P(("wide", "narrow"), None),
        P(),
        P(),
        P(),
        P(),
        P(),
        P(None, "narrow"),
        P("narrow"),
        P("narrow", None),
        P(),
        P(("wide", "narrow"), None),
    )
    out_specs = (
        P(("wide", "narrow"), None),
        P(("wide", "narrow"), None),
        P("narrow"),
        P("narrow"),
        P(None, "narrow"),
        P("narrow"),
        P("narrow", None),
        P(None, "narrow"),
        P("narrow"),
        P("narrow", None),
        P("narrow"),
    )
    return jax.shard_map(
        make_body(mesh.shape["wide"]), mesh=mesh, in_specs=in_specs, out_specs=out_specs, check_vma=False)
```

```python
import functools
import math

import jax
import jax.numpy as jnp
from jax import lax
from jax.experimental import pallas as pl
from jax.experimental.pallas import tpu as pltpu
from jax.sharding import PartitionSpec as P

D = 1024
HEADS = 16
HEAD = 64
ROT = 16
TILE = 256
PAIR = 2 * HEAD
MAX_DOC = 512
MESH = pl.DeviceIdType.MESH

MLP, DENSE, QKV, BLOCKS, GAP = 8, 8, 9, 12, 8
F_RING, Y_RING, S_RING = 8, 6, 2
LAGS = (4, 5, 6, 7, 8, 9)
CORE, YAXIS, XHALF, NEAR, BACK, WIDE_A, WIDE_B, KINDS = range(8)
ORDER = (3, 1, 2, 0)


def doc_starts(segments):
    return jnp.sum((segments[:, :, None] > segments[:, None, :]).astype(jnp.int32), axis=2)


def rope_tables(position):
    half_rot = ROT // 2
    lane = jnp.arange(PAIR, dtype=jnp.int32) % HEAD
    inv_freq = 1.0 / 10000.0 ** ((lane % half_rot).astype(jnp.float32) * 2.0 / ROT)
    angles = position.astype(jnp.float32)[:, None] * inv_freq[None, :]
    rotated = (lane < ROT)[None, :]
    sin = jnp.where((lane < half_rot)[None, :], -jnp.sin(angles), jnp.sin(angles))
    return jnp.where(rotated, jnp.cos(angles), 1.0), jnp.where(rotated, sin, 0.0)


def turn(t, same, partner):
    half_rot = ROT // 2
    lane = lax.broadcasted_iota(jnp.int32, t.shape, 1) % HEAD
    other = jnp.where(
        lane < half_rot,
        pltpu.roll(t, PAIR - half_rot, axis=1),
        pltpu.roll(t, half_rot, axis=1),
    )
    return t * same + other * partner


def dot_nt(left, right):
    return lax.dot_general(
        left, right, (((1,), (1,)), ((), ())), preferred_element_type=jnp.float32
    )


def dot_nn(left, right):
    return lax.dot_general(
        left, right, (((1,), (0,)), ((), ())), preferred_element_type=jnp.float32
    )


def xor2(value, other):
    return (value + other) % 2 + 2 * ((value // 2 + other // 2) % 2)


def gelu_parts(x):
    cdf = 0.5 * (1.0 + lax.erf(x * math.sqrt(0.5)))
    density = jnp.exp(-0.5 * x * x) * (1.0 / math.sqrt(2.0 * math.pi))
    return x * cdf, cdf + x * density


def widen(value):
    return value.astype(jnp.float32)


def low(value):
    return value.astype(jnp.bfloat16)


def block_of(v):
    late = MLP + GAP
    if isinstance(v, int):
        return (v if v < MLP else v - GAP), 0 <= v < MLP or late <= v < BLOCKS + GAP
    return (
        jnp.where(v < MLP, v, v - GAP),
        ((v >= 0) & (v < MLP)) | ((v >= late) & (v < BLOCKS + GAP)),
    )


def main_kernel(
    wide,
    tokens,
    cot,
    w_qkv,
    w_dense,
    w_up,
    w_down,
    same_in,
    partner_in,
    bias_in,
    start_ref,
    gain,
    ln_bias,
    b_qkv,
    out_bias,
    mixed_out,
    dtok_out,
    straight_out,
    turned_out,
    small_out,
    qkvg,
    att,
    gp,
    core_up,
    core_down,
    y_up,
    y_down,
    diag_up,
    diag_down,
    nrm,
    nrm_t,
    ct,
    ct_t,
    hid,
    gpre,
    pool,
    mixed_acc,
    gn_acc,
    slope,
    s_ring,
    a_ring,
    f_ring,
    r_ring,
    ry,
    rx,
    rz,
    rfar,
    gz,
    gx,
    tbuf,
    bias,
    sv,
    sv_sum,
    sv_recv,
    send,
    recv,
    far_send,
    far_recv,
    sv_send,
    sv_rsem,
    gy_send,
    gy_recv,
    gw_send,
    gw_recv,
    gc_send,
    gc_recv,
    gb_send,
    gb_recv,
    load,
    load_w,
    load_a,
    out_sem,
    free,
    y_free,
):
    rows = nrm.shape[0]
    R_RING, A_RING = r_ring.shape[0], a_ring.shape[0]
    n, w = lax.axis_index("narrow"), lax.axis_index("wide")
    near = w % 4
    xbit, zbit = w % 2, (w // 2) % 2
    bits = [b for b in range(2, 20) if (1 << b) < wide]
    mate = {"narrow": n + 1 - 2 * (n % 2)}
    ymate = {"narrow": n + 2 - 4 * (n // 2)}

    def across(bit):
        return {"wide": w + (1 << bit) - (2 << bit) * ((w // (1 << bit)) % 2)}

    def near_mate(k):
        return {"wide": w - near + xor2(near, k)}

    def spot(r):
        return xor2(n, r)

    def tiles(start, size=TILE):
        return pl.ds(pl.multiple_of(start, TILE), size)

    def remote_to(src, dst, send_sem, recv_sem, dev):
        return pltpu.make_async_remote_copy(
            src_ref=src,
            dst_ref=dst,
            send_sem=send_sem,
            recv_sem=recv_sem,
            device_id=dev,
            device_id_type=MESH,
        )

    def copy_in(src, dst, i):
        return pltpu.make_async_copy(src, dst, load.at[i])

    firsts = [
        copy_in(tokens, hid, 0),
        copy_in(same_in, slope.at[:, 2 * PAIR : 3 * PAIR], 1),
        copy_in(partner_in, slope.at[:, 3 * PAIR : 4 * PAIR], 2),
        copy_in(w_qkv.at[:, 0:rows], pool.at[1], 3),
        copy_in(w_qkv.at[:, rows : 2 * rows], pool.at[2], 4),
        copy_in(w_qkv.at[:, 2 * rows : 3 * rows], pool.at[3], 5),
        copy_in(w_dense, pool.at[0], 6),
        copy_in(cot, ct, 7),
    ]
    own_bias = copy_in(bias_in, bias.at[0], 8)
    for c in firsts:
        c.start()
    own_bias.start()

    partners = [mate, ymate, near_mate(3)] + [across(b) for b in [0, 1] + bits]
    barrier = pltpu.get_barrier_semaphore()
    for p in partners:
        pl.semaphore_signal(barrier, inc=1, device_id=p, device_id_type=MESH)
    pl.semaphore_wait(barrier, len(partners))

    def gather_y(k, a):
        if k == 0:
            src, dst = w_up.at[tiles(near * TILE), tiles(a * TILE)], y_up.at[a, tiles(near * TILE)]
        else:
            src = w_down.at[tiles(a * TILE), tiles(near * TILE)]
            dst = y_down.at[a, :, tiles(near * TILE)]
        return remote_to(src, dst, gy_send.at[k, a], gy_recv.at[k, a], ymate)

    def gather_near(k, a, to):
        ref = y_up.at[a, tiles(near * TILE)] if k == 0 else y_down.at[a, :, tiles(near * TILE)]
        return remote_to(
            ref, ref, gw_send.at[k, a, to - 1], gw_recv.at[k, a, to - 1], near_mate(to)
        )

    def gather_core(k, a):
        src = (
            w_up.at[:, tiles(a * TILE)],
            w_down.at[tiles(a * TILE)],
            y_up.at[a],
            y_down.at[a],
        )[k]
        dst = (core_up, core_down, diag_up, diag_down)[k].at[a]
        return remote_to(src, dst, gc_send.at[k, a], gc_recv.at[k, a], mate)

    def gather_bias(i):
        src = (0, 0, 2)[i]
        dst = (1, 2, 3)[i]
        dev = (mate, ymate, mate)[i]
        return remote_to(bias.at[src], bias.at[dst], gb_send.at[i], gb_recv.at[i], dev)

    def arrived_y(a):
        for k in range(2):
            gather_y(k, a).wait_recv()
            for to in (1, 2, 3):
                gather_near(k, a, to).start()

    def arrived_near(a):
        for k in range(2):
            for to in (1, 2, 3):
                gather_near(k, a, to).wait_recv()
            gather_core(2 + k, a).start()

    def weights(a):
        slot = a % 2
        copies = []
        for p, r in enumerate(ORDER):
            src = (
                (w_up.at[:, tiles(a * TILE)], w_down.at[tiles(a * TILE)]),
                (core_up.at[a], core_down.at[a]),
                (y_up.at[a], y_down.at[a]),
                (diag_up.at[a], diag_down.at[a]),
            )[r]
            cols = slice(p * TILE, (p + 1) * TILE)
            copies.append(
                pltpu.make_async_copy(src[0], pool.at[2 * slot, :, cols], load_w.at[slot, p])
            )
            copies.append(
                pltpu.make_async_copy(src[1], pool.at[2 * slot + 1, cols], load_w.at[slot, 4 + p])
            )
        return copies

    def weights_here(a):
        for k in range(4):
            gather_core(k, a).wait_recv()
        for c in weights(a):
            c.start()

    for a in range(4):
        for k in range(2):
            gather_y(k, a).start()
            gather_core(k, a).start()
    own_bias.wait()
    gather_bias(0).start()
    gather_bias(1).start()

    sv[...] = jnp.zeros_like(sv)
    firsts[0].wait()

    def norm(m, c):
        at = tiles(m * TILE)
        x = widen(hid[at, :])
        mean = jnp.mean(x, axis=-1, keepdims=True)
        centered = x - mean
        variance = jnp.mean(centered * centered, axis=-1, keepdims=True)
        normed = centered * lax.rsqrt(variance + 1e-05) * gain[...] + ln_bias[...]
        nrm[at, :] = low(normed)
        nrm_t[:, at] = low(normed.T)
        return c

    lax.fori_loop(0, rows // TILE, norm, 0)
    half = rows // 2

    def store_out(i, buf):
        return pltpu.make_async_copy(buf, qkvg.at[i], load.at[i])

    buffers = (hid, gpre, hid, gpre)
    for i in range(4):
        buf = buffers[i]
        if i == 0:
            firsts[1].wait()
            firsts[2].wait()
        if i >= 2:
            store_out(i - 2, buf).wait()
        if i < 3:
            firsts[3 + i].wait()
        else:
            firsts[6].wait()
            firsts[7].wait()

        def project(m, c, i=i, buf=buf):
            at = pl.ds(pl.multiple_of(m * half, half), half)
            if i == 3:
                buf[at, :] = low(dot_nt(ct[at, :], pool[0]))
                return c
            got = dot_nn(nrm[at, :], pool[1 + i]) + b_qkv[0:1, i * rows : (i + 1) * rows]
            if i == 2:
                buf[at, :] = low(got)
                return c
            same, partner = slope[at, 2 * PAIR : 3 * PAIR], slope[at, 3 * PAIR : 4 * PAIR]
            for k in range(0, rows, PAIR):
                t = turn(got[:, k : k + PAIR], same, partner)
                if i == 0:
                    t = t * (1.0 / math.sqrt(HEAD))
                buf[at, k : k + PAIR] = low(t)
            return c

        lax.fori_loop(0, 2, project, 0)
        store_out(i, buf).start()
        if i > 0:
            arrived_y(i - 1)
    gather_bias(1).wait_recv()
    gather_bias(2).start()

    def turn_cot(m, c):
        at = tiles(m * TILE)
        ct_t[:, at] = low(widen(ct[at, :]).T)
        return c

    lax.fori_loop(0, rows // TILE, turn_cot, 0)
    mixed_acc[...] = jnp.zeros_like(mixed_acc)
    gn_acc[...] = jnp.zeros_like(gn_acc)
    arrived_near(0)
    arrived_y(3)
    store_out(2, hid).wait()
    store_out(3, gpre).wait()
    gather_bias(0).wait_recv()
    gather_bias(2).wait_recv()

    quarter = rows // 4
    own_half, other_half = half * xbit, half * (1 - xbit)
    own_q = own_half + quarter * zbit
    other_q = own_half + quarter * (1 - zbit)

    def seg(start, size):
        return pl.ds(pl.multiple_of(start, quarter), size)

    def remote(src, dst, kind, b, dev):
        return remote_to(src, dst, send.at[kind, b], recv.at[kind, b], dev)

    def core_copy(b):
        return remote(s_ring.at[b % S_RING], r_ring.at[b % R_RING], CORE, b, mate)

    def y_copy(b):
        return remote(a_ring.at[b % A_RING], ry.at[b % Y_RING], YAXIS, b, ymate)

    def x_copy(b):
        return remote(f_ring.at[b % F_RING, seg(other_half, half)], rx.at[b], XHALF, b, across(0))

    def z_copy(b):
        return remote(f_ring.at[b % F_RING, seg(other_q, quarter)], rz.at[b], NEAR, b, across(1))

    def far_copy(i, b):
        return remote_to(
            f_ring.at[b % F_RING, seg(own_q, quarter)],
            rfar.at[i, b],
            far_send.at[i, b],
            far_recv.at[i, b],
            across(bits[i]),
        )

    def back_z(b):
        return remote(f_ring.at[b % F_RING, seg(own_q, quarter)], gz.at[b], BACK, b, across(1))

    def back_xa(b):
        return remote(
            f_ring.at[b % F_RING, seg(own_q, quarter)], gx.at[b, 0], WIDE_A, b, across(0)
        )

    def back_xb(b):
        return remote(gz.at[b], gx.at[b, 1], WIDE_B, b, across(0))

    def is_turned(b):
        return (b % 2 == 0) & (b <= DENSE)

    def piece(i, b):
        src = (
            f_ring.at[b % F_RING, seg(own_q, quarter)],
            gz.at[b],
            gx.at[b, 0],
            gx.at[b, 1],
        )[i]
        at = own_half if i < 2 else other_half
        return src, at + quarter * (zbit if i % 2 == 0 else 1 - zbit)

    def straight_copy(i, b):
        src, at = piece(i, b)
        column = jnp.where(b < MLP, b // 2, b - QKV + MLP // 2)
        return pltpu.make_async_copy(
            src, straight_out.at[seg(at, quarter), tiles(column * TILE)], out_sem.at[i, b]
        )

    def turned_copy(i, b):
        src, at = piece(i, b)
        return pltpu.make_async_copy(
            tbuf.at[(b // 2) % 2, i],
            turned_out.at[tiles((b // 2) * TILE), seg(at, quarter)],
            out_sem.at[i, b],
        )

    def put(i, b):
        @pl.when(is_turned(b))
        def _():
            src, at = piece(i, b)
            tbuf[(b // 2) % 2, i] = low(widen(src[...]).T)
            turned_copy(i, b).start()

        @pl.when(jnp.logical_not(is_turned(b)))
        def _():
            straight_copy(i, b).start()

    def add_into(b, start, size, other):
        at = seg(start, size)
        slot = b % F_RING
        f_ring[slot, at] = low(widen(f_ring[slot, at]) + widen(other[...]))

    def stage_y(b):
        y_copy(b).wait_recv()
        add_into(b, other_half, half, ry.at[b % Y_RING, seg(other_half, half)])
        x_copy(b).start()
        add_into(b, own_half, half, ry.at[b % Y_RING, seg(own_half, half)])

        @pl.when(b + Y_RING < BLOCKS)
        def _():
            pl.semaphore_signal(y_free, inc=1, device_id=ymate, device_id_type=MESH)

    def stage_x(b):
        x_copy(b).wait_recv()
        add_into(b, other_q, quarter, rx.at[b, seg(quarter * (1 - zbit), quarter)])
        z_copy(b).start()
        add_into(b, own_q, quarter, rx.at[b, seg(quarter * zbit, quarter)])

    def stage_near(b):
        z_copy(b).wait_recv()
        add_into(b, own_q, quarter, rz.at[b])
        far_copy(0, b).start()

    def stage_far(b):
        for i in range(len(bits)):
            far_copy(i, b).wait()
            add_into(b, own_q, quarter, rfar.at[i, b])
            if i + 1 < len(bits):
                far_copy(i + 1, b).start()
        back_z(b).start()
        back_xa(b).start()
        put(0, b)
        x_copy(b).wait_send()
        z_copy(b).wait_send()

    def stage_back(b):
        back_z(b).wait_recv()
        back_xb(b).start()
        put(1, b)

    def stage_out(b):
        back_xa(b).wait_recv()
        put(2, b)
        back_xb(b).wait_recv()
        put(3, b)
        back_z(b).wait_send()
        back_xa(b).wait_send()
        back_xb(b).wait_send()
        for i in range(4):
            straight_copy(i, b).wait()

    stages = (stage_y, stage_x, stage_near, stage_far, stage_back, stage_out)

    def progress(v):
        for lag, stage in reversed(list(zip(LAGS, stages))):
            b, there = block_of(v - lag)

            @pl.when(there)
            def _(stage=stage, b=b):
                stage(b)

    def parts_away(b, left, right):
        @pl.when(b >= S_RING)
        def _():
            core_copy(b - S_RING).wait_send()

        s_ring[b % S_RING] = low(dot_nn(left[...], right[...]))

        @pl.when(b >= R_RING)
        def _():
            pl.semaphore_wait(free, 1)

        core_copy(b).start()

    def parts_here(b, left, right):
        @pl.when(b >= A_RING)
        def _():
            y_copy(b - A_RING).wait_send()

        core_copy(b).wait_recv()
        got = dot_nn(left[...], right[...]) + widen(r_ring[b % R_RING])
        a_ring[b % A_RING] = low(got[:, :TILE])

        @pl.when(b >= Y_RING)
        def _():
            pl.semaphore_wait(y_free, 1)

        y_copy(b).start()
        f_ring[b % F_RING] = low(got[:, TILE:])

        @pl.when(b + R_RING < BLOCKS)
        def _():
            pl.semaphore_signal(free, inc=1, device_id=mate, device_id_type=MESH)

    def accumulate(target, left, right, dot):
        def chunk(m, c):
            at = pl.ds(pl.multiple_of(m * half, half), half)
            target[at, :] += dot(left[at, :], right[...])
            return c

        lax.fori_loop(0, 2, chunk, 0)

    def in_pair(i, s):
        cols = tiles_pair(i)
        return [
            pltpu.make_async_copy(
                qkvg.at[c, :, cols], pool.at[s, :, c * PAIR : (c + 1) * PAIR], load_a.at[s, c]
            )
            for c in range(4)
        ]

    def tiles_pair(i):
        return pl.ds(pl.multiple_of(i * PAIR, PAIR), PAIR)

    weights_here(0)

    def mlp_block(cb, carry):
        slot = cb % 2
        for c in weights(cb):
            c.wait()

        @pl.when(cb == 3)
        def _():
            for c in in_pair(0, 0):
                c.start()

        for side in range(2):
            cols = slice(side * 2 * TILE, (side + 1) * 2 * TILE)
            up, down = pool.at[2 * slot, :, cols], pool.at[2 * slot + 1, cols]
            at = tiles(cb * TILE)
            bias_row = jnp.concatenate(
                [bias[ORDER[2 * side], 0:1, at], bias[ORDER[2 * side + 1], 0:1, at]], axis=1
            )

            def act(m, c):
                at = pl.ds(pl.multiple_of(m * half, half), half)
                value, grad = gelu_parts(dot_nn(nrm[at, :], up[...]) + bias_row)
                hid[at, cols] = low(value)
                slope[at, :] = grad
                return c

            lax.fori_loop(0, 2, act, 0)
            parts = (parts_away, parts_here)[side]
            parts(2 * cb, ct_t, hid.at[:, cols])
            if side == 0:

                @pl.when(cb < 3)
                def _():
                    arrived_near(cb + 1)

            else:
                progress(2 * cb)

            def back(m, total):
                at = pl.ds(pl.multiple_of(m * half, half), half)
                got = low(dot_nt(ct[at, :], down[...]) * slope[at, :])
                gpre[at, cols] = got
                return total + jnp.sum(widen(got), axis=0, keepdims=True)

            total = lax.fori_loop(0, 2, back, jnp.zeros((1, 2 * TILE), jnp.float32))
            for k in range(2):
                sv[ORDER[2 * side + k], pl.ds(6 + cb, 1), :] = total[:, k * TILE : (k + 1) * TILE]
            parts(2 * cb + 1, nrm_t, gpre.at[:, cols])

        @pl.when(cb < 3)
        def _():
            weights_here(cb + 1)

        accumulate(mixed_acc, hid, pool.at[2 * slot + 1], dot_nn)
        accumulate(gn_acc, gpre, pool.at[2 * slot], dot_nt)
        progress(2 * cb + 1)
        return carry

    lax.fori_loop(0, 4, mlp_block, 0)

    tables = [
        copy_in(same_in, slope.at[:, 2 * PAIR : 3 * PAIR], 0),
        copy_in(partner_in, slope.at[:, 3 * PAIR : 4 * PAIR], 1),
    ]
    for c in tables:
        c.start()

    def ordered(j, ref, i, by_rows):
        copies = []
        for p, r in enumerate(ORDER):
            cols = slice(p * TILE, (p + 1) * TILE)
            if by_rows:
                src, dst = w_dense.at[tiles(spot(r) * TILE)], ref.at[cols]
            else:
                src, dst = w_qkv.at[:, tiles((3 * spot(r) + j) * TILE)], ref.at[:, cols]
            copies.append(pltpu.make_async_copy(src, dst, load_w.at[i, p]))
        return copies

    later = [ordered(0, hid, 0, False), ordered(1, gpre, 1, False)]
    for group in later:
        for c in group:
            c.start()
    for c in tables:
        c.wait()

    def out_pair(i, s):
        cols = tiles_pair(i)
        dsts = [att.at[:, cols]] + [gp.at[c, :, cols] for c in range(3)]
        return [
            pltpu.make_async_copy(
                pool.at[s, :, (4 + c) * PAIR : (5 + c) * PAIR], dsts[c], load_a.at[s, 4 + c]
            )
            for c in range(4)
        ]

    def attention(i, carry):
        s = i % 2
        for c in in_pair(i, s):
            c.wait()

        @pl.when(i + 1 < GAP)
        def _():
            for c in in_pair(i + 1, 1 - s):
                c.start()

        @pl.when(i >= 2)
        def _():
            for c in out_pair(i - 2, s):
                c.wait()

        def view(c):
            return pool.at[s, :, c * PAIR : (c + 1) * PAIR]

        q_ref, k_ref, v_ref, g_ref, att_ref, dq_ref, dk_ref, dv_ref = map(view, range(8))
        kt_ref, vt_ref = pool.at[2, 0:PAIR], pool.at[2, PAIR : 2 * PAIR]
        dk_acc, dv_acc = slope.at[:, 0:PAIR], slope.at[:, PAIR : 2 * PAIR]
        same_ref, partner_ref = (
            slope.at[:, 2 * PAIR : 3 * PAIR],
            slope.at[:, 3 * PAIR : 4 * PAIR],
        )
        lane = lax.broadcasted_iota(jnp.int32, (1, PAIR), 1)
        dk_acc[...] = jnp.zeros((rows, PAIR), jnp.float32)
        dv_acc[...] = jnp.zeros((rows, PAIR), jnp.float32)
        kt_ref[...] = low(widen(k_ref[...]).T)
        vt_ref[...] = low(widen(v_ref[...]).T)
        for block in range(rows // TILE):
            first = max(0, block - MAX_DOC // TILE)
            here = slice(block * TILE, (block + 1) * TILE)
            q_pair, g_pair = q_ref[here, :], g_ref[here, :]
            start = start_ref[:, here]
            query_index = block * TILE + lax.broadcasted_iota(jnp.int32, (1, TILE), 1)
            keys = [slice(j * TILE, (j + 1) * TILE) for j in range(first, block + 1)]
            visible = []
            for k in keys:
                index = k.start + lax.broadcasted_iota(jnp.int32, (TILE, TILE), 0)
                seen = index >= start
                visible.append(seen & (index <= query_index) if k.start == here.start else seen)
            out_t, dq_t = [], []
            for head in range(2):
                mine = (lane >= head * HEAD) & (lane < (head + 1) * HEAD)
                q = jnp.where(mine, q_pair, jnp.zeros_like(q_pair))
                g = jnp.where(mine, g_pair, jnp.zeros_like(g_pair))
                span = slice(head * HEAD, (head + 1) * HEAD)
                scores = [
                    jnp.where(see, dot_nt(k_ref[k, :], q), -1e30) for k, see in zip(keys, visible)
                ]
                grad_prob = [dot_nt(v_ref[k, :], g) for k in keys]
                top = functools.reduce(
                    jnp.maximum, [jnp.max(t, axis=0, keepdims=True) for t in scores]
                )
                exps = [jnp.exp(t - top) for t in scores]
                inverse = 1.0 / sum(jnp.sum(e, axis=0, keepdims=True) for e in exps)
                probs = [e * inverse for e in exps]
                row_dot = sum(
                    jnp.sum(p * d, axis=0, keepdims=True) for p, d in zip(probs, grad_prob)
                )
                out_head = jnp.zeros((HEAD, TILE), jnp.float32)
                dq_head = jnp.zeros((HEAD, TILE), jnp.float32)
                for k, p, d in zip(keys, probs, grad_prob):
                    p_low = low(p)
                    grad_score = low(p * (d - row_dot))
                    out_head += dot_nn(vt_ref[span, k], p_low)
                    dq_head += dot_nn(kt_ref[span, k], grad_score)
                    dv_acc[k, :] += dot_nn(p_low, g)
                    dk_acc[k, :] += dot_nn(grad_score, q)
                out_t.append(out_head)
                dq_t.append(dq_head)
            att_ref[here, :] = low(jnp.concatenate(out_t, axis=0).T)
            dq = jnp.concatenate(dq_t, axis=0).T * (1.0 / math.sqrt(HEAD))
            dq_ref[here, :] = low(turn(dq, same_ref[here, :], -partner_ref[here, :]))
        dk_ref[...] = low(turn(dk_acc[...], same_ref[...], -partner_ref[...]))
        dv_ref[...] = low(dv_acc[...])
        for c in out_pair(i, s):
            c.start()
        progress(MLP + i)
        return carry

    lax.fori_loop(0, GAP, attention, 0)
    for i in (GAP - 2, GAP - 1):
        for c in out_pair(i, i % 2):
            c.wait()

    def att_tiles():
        return [
            pltpu.make_async_copy(
                att.at[:, tiles(spot(r) * TILE)],
                pool.at[0, :, p * TILE : (p + 1) * TILE],
                load_w.at[2, p],
            )
            for p, r in enumerate(ORDER)
        ]

    def gp_tiles(j):
        copies = []
        for p, r in enumerate(ORDER):
            at = 3 * spot(r) + j
            copies.append(
                pltpu.make_async_copy(
                    gp.at[at // 4, :, tiles((at % 4) * TILE)],
                    pool.at[1 + j, :, p * TILE : (p + 1) * TILE],
                    load_w.at[3, 4 * j + p],
                )
            )
        return copies

    for c in att_tiles():
        c.start()
    for j in range(3):
        for c in gp_tiles(j):
            c.start()
    pair_a, pair_b = slice(0, 2 * TILE), slice(2 * TILE, 4 * TILE)
    for c in att_tiles():
        c.wait()
    parts_away(DENSE, ct_t, pool.at[0, :, pair_a])
    parts_here(DENSE, ct_t, pool.at[0, :, pair_b])
    progress(DENSE + GAP)

    def qkv_block(j, carry):
        for c in gp_tiles(j):
            c.wait()
        parts_away(QKV + j, nrm_t, pool.at[1 + j, :, pair_a])
        parts_here(QKV + j, nrm_t, pool.at[1 + j, :, pair_b])
        total = jnp.sum(widen(pool[1 + j]), axis=0, keepdims=True)
        for p, r in enumerate(ORDER):
            sv[r, pl.ds(3 + j, 1), :] = total[:, p * TILE : (p + 1) * TILE]
        progress(QKV + GAP + j)
        return carry

    lax.fori_loop(0, 3, qkv_block, 0)
    for group in later:
        for c in group:
            c.wait()
    accumulate(gn_acc, pool.at[1], hid, dot_nt)
    accumulate(gn_acc, pool.at[2], gpre, dot_nt)
    last = ordered(2, hid, 0, False) + ordered(0, gpre, 1, True)
    tok_load = copy_in(tokens, pool.at[1], 0)
    for c in last + [tok_load]:
        c.start()
    for c in last:
        c.wait()
    accumulate(gn_acc, pool.at[3], hid, dot_nt)
    accumulate(mixed_acc, pool.at[0], gpre, dot_nn)
    tok_load.wait()
    tick = BLOCKS + GAP
    progress(tick)

    def finish(m, sums):
        at = tiles(m * TILE)
        x = widen(pool[1, at, :])
        mean = jnp.mean(x, axis=-1, keepdims=True)
        centered = x - mean
        variance = jnp.mean(centered * centered, axis=-1, keepdims=True)
        inv_std = lax.rsqrt(variance + 1e-05)
        unit = centered * inv_std
        hid[at, :] = low(mixed_acc[at, :] + x + out_bias[...])
        gn = gn_acc[at, :]
        g = gn * gain[...]
        mean_grad = jnp.mean(g, axis=-1, keepdims=True)
        mean_proj = jnp.mean(g * unit, axis=-1, keepdims=True)
        c = widen(ct[at, :])
        gpre[at, :] = low(c + inv_std * (g - mean_grad - unit * mean_proj))
        return (
            sums[0] + jnp.sum(gn * unit, axis=0, keepdims=True),
            sums[1] + jnp.sum(gn, axis=0, keepdims=True),
            sums[2] + jnp.sum(c, axis=0, keepdims=True),
        )

    zero = jnp.zeros((1, rows), jnp.float32)
    sums = lax.fori_loop(0, rows // TILE, finish, (zero, zero, zero))
    final = [
        pltpu.make_async_copy(hid, mixed_out, load.at[1]),
        pltpu.make_async_copy(gpre, dtok_out, load.at[2]),
    ]
    for c in final:
        c.start()
    for i in range(3):
        sv_sum[i : i + 1, :] = sums[i]
    for r in range(4):
        sv[r, 0:3, :] = sv_sum[0:3, tiles(spot(r) * TILE)]

    def sv_copy(i, src, dev):
        return remote_to(src, sv_recv.at[i], sv_send.at[i], sv_rsem.at[i], dev)

    hops = [
        sv_copy(0, sv.at[1], mate),
        sv_copy(1, sv.at[3], mate),
        sv_copy(2, sv.at[2], ymate),
    ]
    hops += [sv_copy(3 + i, sv.at[0], across(b)) for i, b in enumerate([0, 1] + bits)]
    hops[0].start()
    hops[1].start()
    tick += 1
    progress(tick)
    hops[0].wait()
    hops[1].wait()
    sv[0] = sv[0] + sv_recv[0]
    sv[2] = sv[2] + sv_recv[1]
    hops[2].start()
    tick += 1
    progress(tick)
    hops[2].wait()
    sv[0] = sv[0] + sv_recv[2]
    for i in range(3, len(hops)):
        hops[i].start()
        tick += 1
        if tick < BLOCKS + GAP + LAGS[-1]:
            progress(tick)
        hops[i].wait()
        sv[0] = sv[0] + sv_recv[i]
    small_out[...] = sv[0]
    while tick + 1 < BLOCKS + GAP + LAGS[-1]:
        tick += 1
        progress(tick)

    for c in final:
        c.wait()
    for b in range(BLOCKS - S_RING, BLOCKS):
        core_copy(b).wait_send()
    for b in range(BLOCKS - A_RING, BLOCKS):
        y_copy(b).wait_send()
    for i in range(3):
        gather_bias(i).wait_send()
    for a in range(4):
        for k in range(2):
            gather_y(k, a).wait_send()
            for to in (1, 2, 3):
                gather_near(k, a, to).wait_send()
        for k in range(4):
            gather_core(k, a).wait_send()


def main_call(wide, hbm_args, vmem_args):
    tokens = hbm_args[0]
    rows, width = tokens.shape
    hops = max(wide.bit_length() - 1, 2)
    far = hops - 2
    bf, f32 = jnp.bfloat16, jnp.float32
    half, quarter = rows // 2, rows // 4
    vm = pltpu.VMEM
    dma = pltpu.SemaphoreType.DMA
    shape = jax.ShapeDtypeStruct
    any_space, vmem_space = (pl.BlockSpec(memory_space=s) for s in (pl.ANY, pltpu.VMEM))
    return pl.pallas_call(
        functools.partial(main_kernel, wide),
        in_specs=[any_space] * len(hbm_args) + [vmem_space] * len(vmem_args),
        out_specs=[any_space] * 4 + [vmem_space] + [any_space] * 9,
        out_shape=[
            shape((rows, width), bf),
            shape((rows, width), bf),
            shape((width, 7 * TILE), bf),
            shape((5 * TILE, width), bf),
            shape((16, TILE), f32),
            shape((4, rows, width), bf),
            shape((rows, width), bf),
            shape((3, rows, width), bf),
        ]
        + [shape((4, width, TILE), bf), shape((4, TILE, width), bf)] * 3,
        scratch_shapes=[
            vm((rows, width), bf),
            vm((width, rows), bf),
            vm((rows, width), bf),
            vm((width, rows), bf),
            vm((rows, width), bf),
            vm((rows, width), bf),
            vm((4, rows, width), bf),
            vm((rows, width), f32),
            vm((rows, width), f32),
            vm((rows, 2 * TILE), f32),
            vm((S_RING, width, 2 * TILE), bf),
            vm((4 if far < 2 else 2, width, TILE), bf),
            vm((F_RING, width, TILE), bf),
            vm((2, width, 2 * TILE), bf),
            vm((Y_RING, width, TILE), bf),
            vm((BLOCKS, half, TILE), bf),
            vm((BLOCKS, quarter, TILE), bf),
            vm((far, BLOCKS, quarter, TILE), bf),
            vm((BLOCKS, quarter, TILE), bf),
            vm((BLOCKS, 2, quarter, TILE), bf),
            vm((2, 4, TILE, TILE), bf),
            vm((4, 8, width), f32),
            vm((4, 16, TILE), f32),
            vm((8, width), f32),
            vm((3 + hops, 16, TILE), f32),
            dma((KINDS, BLOCKS)),
            dma((KINDS, BLOCKS)),
            dma((far, BLOCKS)),
            dma((far, BLOCKS)),
            dma((3 + hops,)),
            dma((3 + hops,)),
            dma((2, 4)),
            dma((2, 4)),
            dma((2, 4, 3)),
            dma((2, 4, 3)),
            dma((4, 4)),
            dma((4, 4)),
            dma((3,)),
            dma((3,)),
            dma((9,)),
            dma((4, 12)),
            dma((2, 8)),
            dma((4, BLOCKS)),
            pltpu.SemaphoreType.REGULAR,
            pltpu.SemaphoreType.REGULAR,
        ],
        compiler_params=pltpu.CompilerParams(
            collective_id=0, has_side_effects=True, vmem_limit_bytes=62 << 20
        ),
        cost_estimate=pl.CostEstimate(
            flops=90 * rows * width * width, bytes_accessed=100 << 20, transcendentals=0
        ),
    )(*hbm_args, *vmem_args)


def make_body(wide):
    def body(
        tokens,
        seg_ids,
        ln_gain,
        ln_bias,
        w_qkv,
        b_qkv,
        w_dense,
        w_up,
        b_up,
        w_down,
        out_bias,
        cotangent,
    ):
        seq_len = seg_ids.shape[1]
        starts = doc_starts(seg_ids)
        position = jnp.arange(seq_len, dtype=jnp.int32) - starts[0]
        same, partner = rope_tables(position)

        def row(vector):
            return vector.astype(jnp.float32)[None, :]

        bias_rows = jnp.broadcast_to(row(b_up), (8, b_up.shape[0]))
        mixed, d_tokens, straight, turned, small = main_call(
            wide,
            (tokens, cotangent, w_qkv, w_dense, w_up, w_down, same, partner, bias_rows),
            (starts, row(ln_gain), row(ln_bias), row(b_qkv), row(out_bias)),
        )[:5]
        split = MLP // 2 * TILE
        return (
            mixed,
            d_tokens,
            small[0],
            small[1],
            straight[:, split:].astype(jnp.float32),
            small[3:6].reshape(-1),
            turned[split:].astype(jnp.float32),
            straight[:, :split].astype(jnp.float32),
            small[6:10].reshape(-1),
            turned[:split].astype(jnp.float32),
            small[2],
        )

    return body


def solution(mesh):
    in_specs = (
        P(("wide", "narrow"), None),
        P(("wide", "narrow"), None),
        P(),
        P(),
        P(),
        P(),
        P(),
        P(None, "narrow"),
        P("narrow"),
        P("narrow", None),
        P(),
        P(("wide", "narrow"), None),
    )
    out_specs = (
        P(("wide", "narrow"), None),
        P(("wide", "narrow"), None),
        P("narrow"),
        P("narrow"),
        P(None, "narrow"),
        P("narrow"),
        P("narrow", None),
        P(None, "narrow"),
        P("narrow"),
        P("narrow", None),
        P("narrow"),
    )
    return jax.shard_map(
        make_body(mesh.shape["wide"]), mesh=mesh, in_specs=in_specs, out_specs=out_specs, check_vma=False)
```
